32 devices in a mesh: grp: 2 (over y), row: 8 (over z, x), col: 2 (over core).
Axes of the slice: x: 2, y: 2, z: 4, core: 2. Of those that a mesh axis runs over, the one named last changes fastest.
Arguments:
- normed_features: bfloat16 [64, 32, 256], P(('grp', 'col'), 'row'), parts along dimension 0, may hold values from -6 to 6
- alignment_mask: int32 [64, 32], P(('grp', 'col'), 'row'), parts along dimension 0, may hold values from 0 to 1, as said below
- residue_present_mask: int32 [64], P(('grp', 'row')), parts along dimension 0, may hold values from 0 to 1
- first_factor_matrix: bfloat16 [256, 32], replicated, may hold values from -0.375 to 0.375
- second_factor_matrix: bfloat16 [256, 32], replicated, may hold values from -0.375 to 0.375
- output_weight: bfloat16 [1024, 128], replicated, may hold values from -0.75 to 0.75
- pairwise_bias: float32 [128], replicated, may hold values from -3 to 3
- cotangent: bfloat16 [64, 32, 128], P(('grp', 'row'), 'col'), parts along dimension 0, may hold values from -0.72 to 0.72
Outputs:
- pair_update: bfloat16 [64, 32, 128], P(('grp', 'row'), 'col'), parts along dimension 0
- left_grad: float32 [64, 32, 32], P(('grp', 'col'), 'row'), parts along dimension 0
- right_grad: float32 [64, 32, 32], P(('grp', 'col'), 'row'), parts along dimension 0
The draws below stay inside these ranges and needn't reach their ends.
There are 2 independent parts, one for each index of `grp`. The reference program is written for one: setup_inputs(seed, part) draws one part's arguments, and reference() takes and returns one part's arrays. A program takes and returns all parts, laid end to end along the dimension named above; an argument that names none is the same for every part. Nothing has to cross between parts.
Inputs may be any that keep to these rules, and one draw needn't show every extreme that they name: `alignment_mask`: 0 or 1; sequence 0 (the query) is present at every residue.
All inputs are finite; a program needn't handle non-finite values.
Results may differ from the reference program's by a relative error of at most 0.006.
Values may be sent and summed in bfloat16 or wider, within the bound.
A program may use at most 64 MiB of HBM per device.

```python
import math
import jax
import jax.numpy as jnp
from jax import lax

FEATURE_DEPTH = 256
PROJ_DEPTH = 32
CZ = 128
RES_DEV = 4
ALIGNED_CHAINS = 32
CUT_POSITIONS = 32


def draw_alignment_mask(key, part):
    chain_number = jnp.arange(ALIGNED_CHAINS, dtype=jnp.int32)[:, None]
    upper_cap = 30 + 65 * chain_number // max(ALIGNED_CHAINS - 1, 1)
    cyclic_shifted = jax.random.randint(jax.random.fold_in(key, 17), (ALIGNED_CHAINS, CUT_POSITIONS), 0, 100, dtype=jnp.int32)
    present = (cyclic_shifted < upper_cap).astype(jnp.int32)
    return jnp.where(chain_number == 0, 1, present).astype(jnp.int32)


def present_residues(key):
    picks = jax.random.randint(jax.random.fold_in(key, 29), (CUT_POSITIONS,), 0, 8, dtype=jnp.int32)
    return (picks < 7).astype(jnp.int32)


def draw_residue_present_mask(key, part):
    return present_residues(key)


def draw_cotangent(key, part):
    present = present_residues(key).astype(jnp.float32)
    noise_key = jax.random.fold_in(key, 41)
    shape = (CUT_POSITIONS, CUT_POSITIONS, CZ)
    base = jnp.clip(jax.random.normal(noise_key, shape, jnp.float32), -6.0, 6.0)
    block_order = jax.random.permutation(jax.random.fold_in(key, 53), CUT_POSITIONS // RES_DEV)
    block_number = jnp.arange(CUT_POSITIONS, dtype=jnp.int32) // RES_DEV
    paired = block_order[block_number][:, None] == block_number[None, :]
    boost = jnp.where(paired, 4.0, 1.0)
    pair_live = present[:, None] * present[None, :]
    weight = boost * (0.08 + 0.92 * pair_live)
    return (0.03 * base * weight[:, :, None]).astype(jnp.bfloat16)


def shard_levels(own_key, shape, pieces, least, high):
    loudness, own = 1.0, jax.random.fold_in(own_key, 6)
    for axis_at, shards_of in pieces:
        heights = jnp.exp(jax.random.uniform(jax.random.fold_in(own, axis_at), (shards_of,), jnp.float32, least / len(pieces), high / len(pieces)))
        loudness = loudness * jnp.repeat(heights, shape[axis_at] // shards_of).reshape([-1 if axis == axis_at else 1 for axis in range(len(shape))])
    return loudness


def centred(own_key, shape, width, most, shards=(), held_as=jnp.bfloat16):
    array = jax.random.normal(own_key, shape, jnp.float32) * width
    if len(shards) > 0:
        array = shard_levels(own_key, shape, shards, -0.22, 0.18) * array
    return jnp.clip(array, min=-most, max=most).astype(held_as)


def setup_inputs(seed: int = 0, part: int = 0) -> dict:
    seeds = jax.random.split(jax.random.key(seed), 9)
    part_splits = jax.random.split(jax.random.fold_in(seeds[8], part), 9)
    normed_features = centred(part_splits[0], (ALIGNED_CHAINS, CUT_POSITIONS, FEATURE_DEPTH), 1.0, 6.0, ((0, 2), (1, 8)))
    alignment_mask = draw_alignment_mask(jax.random.fold_in(jax.random.fold_in(seeds[8], part), 71), part)
    residue_present_mask = draw_residue_present_mask(jax.random.fold_in(jax.random.fold_in(seeds[8], part), 71), part)
    first_factor_matrix = centred(seeds[3], (FEATURE_DEPTH, PROJ_DEPTH), FEATURE_DEPTH ** -0.5, 0.375)
    second_factor_matrix = centred(seeds[4], (FEATURE_DEPTH, PROJ_DEPTH), FEATURE_DEPTH ** -0.5, 0.375)
    output_weight = centred(seeds[5], (PROJ_DEPTH * PROJ_DEPTH, CZ), (PROJ_DEPTH * PROJ_DEPTH // 16) ** -0.5, 0.75)
    pairwise_bias = centred(seeds[6], (CZ,), 0.5, 3.0, (), jnp.float32)
    cotangent = draw_cotangent(jax.random.fold_in(jax.random.fold_in(seeds[8], part), 71), part)
    return {"normed_features": normed_features, "alignment_mask": alignment_mask, "residue_present_mask": residue_present_mask, "first_factor_matrix": first_factor_matrix, "second_factor_matrix": second_factor_matrix, "output_weight": output_weight, "pairwise_bias": pairwise_bias, "cotangent": cotangent}


def reference(normed_features, alignment_mask, residue_present_mask, first_factor_matrix, second_factor_matrix, output_weight, pairwise_bias, cotangent):
    sequence_count = normed_features.shape[0]
    residue_count = normed_features.shape[1]
    proj_width = first_factor_matrix.shape[1]
    channels = output_weight.shape[1]
    present_entry_mask = alignment_mask.astype(jnp.float32) * residue_present_mask.astype(jnp.float32)[None, :]
    activation_broad = normed_features.astype(jnp.float32)
    left_proj = (jnp.einsum("srk,kc->src", activation_broad, first_factor_matrix.astype(jnp.float32)) * present_entry_mask[:, :, None]).astype(jnp.bfloat16)
    right_proj = (jnp.einsum("srk,kc->src", activation_broad, second_factor_matrix.astype(jnp.float32)) * present_entry_mask[:, :, None]).astype(jnp.bfloat16)
    pair_count = jnp.dot(present_entry_mask.T, present_entry_mask, precision=lax.Precision.HIGHEST)
    divisor = jnp.maximum(pair_count, 1.0)
    row_block = math.gcd(residue_count, 32)
    num_blocks = residue_count // row_block
    right_wide = right_proj.astype(jnp.float32)

    def per_block(running, block_idx):
        offset = (block_idx * row_block).astype(jnp.int32)
        left_blk = lax.dynamic_slice_in_dim(left_proj, offset, row_block, 1).astype(jnp.float32)
        div_blk = lax.dynamic_slice_in_dim(divisor, offset, row_block, 0)
        cot_blk = lax.dynamic_slice_in_dim(cotangent, offset, row_block, 0)
        products = jnp.einsum("sic,sje->ijce", left_blk, right_wide).astype(jnp.bfloat16)
        products = products.reshape(row_block * residue_count, proj_width * proj_width)
        mapped = jnp.dot(products, output_weight, preferred_element_type=jnp.float32).reshape(row_block, residue_count, channels)
        pair_blk = (mapped / div_blk[:, :, None] + pairwise_bias[None, None, :]).astype(jnp.bfloat16)
        scaled = (cot_blk.astype(jnp.float32) / div_blk[:, :, None]).astype(jnp.bfloat16).reshape(row_block * residue_count, channels)
        grad_outer = jnp.dot(scaled, output_weight.T, preferred_element_type=jnp.float32).astype(jnp.bfloat16)
        grad_outer = grad_outer.reshape(row_block, residue_count, proj_width, proj_width).astype(jnp.float32)
        left_term = jnp.einsum("ijce,sje->sic", grad_outer, right_wide)
        right_term = jnp.einsum("ijce,sic->sje", grad_outer, left_blk)
        return running + right_term, (pair_blk, left_term)

    start_grad = jnp.zeros((sequence_count, residue_count, proj_width), jnp.float32)
    right_grad, (pairs, left_terms) = lax.scan(per_block, start_grad, jnp.arange(num_blocks, dtype=jnp.int32))
    pair_update = pairs.reshape(residue_count, residue_count, channels)
    left_grad = jnp.moveaxis(left_terms, 0, 1).reshape(sequence_count, residue_count, proj_width)
    return pair_update, left_grad, right_grad
```

```python
import functools

import jax
import jax.numpy as jnp
from jax import lax
from jax.experimental import pallas as pl
from jax.experimental.pallas import tpu as pltpu
from jax.sharding import PartitionSpec as P

F32 = jnp.float32
BF16 = jnp.bfloat16
MESH = pl.DeviceIdType.MESH
UNROLL = 8


def iota(shape, axis):
    return lax.broadcasted_iota(jnp.int32, shape, axis)


def mm(a, b):
    return lax.dot_general(a, b, (((1,), (0,)), ((), ())), preferred_element_type=F32)


def each(n, f):
    if n <= UNROLL:
        for k in range(n):
            f(k)
    else:

        @pl.loop(0, n)
        def _(k):
            f(k)


def kernel(
    nrow,
    x_ref, am_ref, rm_ref, wl_ref, wr_ref, w_ref, bias_ref, cot_ref,
    pu_ref, lg_ref, rg_ref,
    g_s, gp_r, f_s, l_r, r_r, ro_r, ct_s, ct_r, cf_r, m_s, m_r,
    w32, a32, b32, o32, c32, p2, q2,
    ssem, rsem, psem,
):
    seq, loc, feat = x_ref.shape
    proj = wl_ref.shape[1]
    half_res, chan = cot_ref.shape[1], cot_ref.shape[2]
    res = nrow * loc
    per_half = half_res // loc
    tiles = proj * seq // 128
    rows = loc * seq
    lo = loc.bit_length() - 1
    sq = seq.bit_length() - 1
    tl = tiles.bit_length() - 1

    grp, row, col = lax.axis_index("grp"), lax.axis_index("row"), lax.axis_index("col")
    other = 1 - col

    def half_of(r):
        return jnp.where(r >= per_half, 1, 0)

    def dev(r, c):
        return (grp, r, c)

    barrier = pltpu.get_barrier_semaphore()

    def greet(k):
        r = lax.rem(row + k, nrow)
        pl.semaphore_signal(barrier, inc=1, device_id=dev(r, other), device_id_type=MESH)
        if isinstance(k, int):
            if k:
                pl.semaphore_signal(barrier, inc=1, device_id=dev(r, col), device_id_type=MESH)
        else:

            @pl.when(k != 0)
            def _():
                pl.semaphore_signal(barrier, inc=1, device_id=dev(r, col), device_id_type=MESH)

    each(nrow, greet)

    xf = x_ref[...].astype(F32)
    x = jnp.concatenate([xf[:, r, :] for r in range(loc)], axis=0).astype(BF16)
    live = jnp.concatenate(
        [(am_ref[:, r : r + 1] * rm_ref[:, r : r + 1]).astype(F32) for r in range(loc)], axis=0
    )
    live = jnp.broadcast_to(live, (rows, 128))
    left = mm(x, wl_ref[...])
    right = mm(x, wr_ref[...])
    both = jnp.concatenate([left, right, jnp.ones((rows, 128 - 2 * proj), F32)], axis=1) * live
    g = both.astype(BF16)
    g_s[...] = g
    lane = iota((rows, 128), 1)
    at = iota((rows, 128), 0)
    m_s[...] = jnp.sum(jnp.where(lane == at, live, 0.0), axis=0, keepdims=True)
    width = 2 * proj * seq
    spread = (iota((128, width), 0) == (iota((128, width), 1) >> sq)).astype(BF16)
    own_seq = (iota((rows, width), 0) & (seq - 1)) == (iota((rows, width), 1) & (seq - 1))
    h = jnp.where(own_seq, mm(g, spread), 0.0).astype(BF16)
    h = jnp.concatenate([h[:, k * 128 : (k + 1) * 128] for k in range(2 * tiles)], axis=0)
    frows, deep = 2 * loc * tiles, 2 * tiles * rows
    fi, ki = iota((frows, deep), 0), iota((frows, deep), 1)
    f_x, f_r, f_t = fi >> (lo + tl), (fi >> tl) & (loc - 1), fi & (tiles - 1)
    k_x, k_t, k_r = ki >> (tl + lo + sq), (ki >> (lo + sq)) & (tiles - 1), (ki >> sq) & (loc - 1)
    pick = ((f_x == k_x) & (f_r == k_r) & (f_t == k_t)).astype(BF16)
    f = mm(pick, h).astype(BF16)
    fr = loc * tiles
    f_s[0] = f[:fr]
    f_s[1] = f[fr:]
    cot32 = cot_ref[...].astype(F32)
    for q in range(per_half if per_half <= UNROLL else 0):
        ct_s[q] = jnp.concatenate(
            [cot32[i, q * loc : (q + 1) * loc, :] for i in range(loc)], axis=0
        ).astype(BF16)
    if per_half > UNROLL:
        c32_rows = c32.shape[0] // loc

        for i in range(loc):
            c32[i * c32_rows : i * c32_rows + half_res] = cot32[i]

        @pl.loop(0, per_half)
        def _(q):
            ct_s[q] = jnp.concatenate(
                [
                    c32[pl.ds(i * c32_rows + q * loc, loc), :]
                    for i in range(loc)
                ],
                axis=0,
            ).astype(BF16)

    pl.semaphore_wait(barrier, 2 * nrow - 1)

    def copy(src, dst, kind, s_slot, r_slot, to):
        return pltpu.make_async_remote_copy(
            src_ref=src, dst_ref=dst, send_sem=ssem.at[kind, s_slot],
            recv_sem=rsem.at[kind, r_slot], device_id=to, device_id_type=MESH,
        )

    def partner(k):
        if k == 0:
            src, dst = g_s, gp_r
        else:
            src, dst = cot_ref, cf_r.at[:, pl.ds(pl.multiple_of(col * half_res, half_res), half_res), :]
        return pltpu.make_async_remote_copy(
            src_ref=src, dst_ref=dst, send_sem=psem.at[k], recv_sem=psem.at[2 + k],
            device_id=dev(row, other), device_id_type=MESH,
        )

    def on(pred, f):
        pl.when(pred)(f)

    def sends(k, act):
        r = lax.rem(row + k, nrow)
        q = jnp.where(r >= per_half, r - per_half, r)
        far = half_of(r) == col

        def same():
            act(copy(f_s.at[1], r_r.at[row], 1, r, row, dev(r, col)))
            act(copy(f_s.at[0], l_r.at[row], 0, r, row, dev(r, col)))
            act(copy(m_s, m_r.at[0, row], 4, r, row, dev(r, col)))
            on(far, lambda: act(copy(ct_s.at[q], ct_r.at[row], 3, r, row, dev(r, col))))

        if isinstance(k, int):
            if k:
                same()
        else:
            on(k != 0, same)
        on(
            half_of(row) == other,
            lambda: act(copy(f_s.at[1], ro_r.at[row], 2, r, row, dev(r, other))),
        )
        act(copy(m_s, m_r.at[1, row], 5, r, row, dev(r, other)))
        on(far, lambda: act(copy(ct_s.at[q], ct_r.at[row], 6, r, row, dev(r, other))))

    partner(0).start()
    partner(1).start()
    each(nrow, lambda j: sends(nrow - 1 - j, lambda d: d.start()))

    l_r[row] = f[:fr]
    r_r[row] = f[fr:]
    m_r[0, row] = m_s[...]
    cf_r[:, pl.ds(pl.multiple_of(col * half_res, half_res), half_res), :] = cot_ref[...]

    @pl.when(half_of(row) == col)
    def _():
        ct_r[row] = ct_s[jnp.where(row >= per_half, row - per_half, row)]

    w32[...] = w_ref[...].astype(F32)
    w_c = jnp.concatenate(
        [w32[pl.ds(e, proj, stride=proj), :] for e in range(proj)], axis=1
    ).astype(BF16)
    w_e = jnp.concatenate(
        [w_ref[c * proj : (c + 1) * proj, :] for c in range(proj)], axis=1
    )

    def spread_left(gl, part):
        p = mm(gl[:, :proj], w_c).astype(BF16)
        for e in range(proj):
            for i in range(loc):
                p2[part * proj * seq + e * seq : part * proj * seq + (e + 1) * seq,
                   i * chan : (i + 1) * chan] = p[
                    i * seq : (i + 1) * seq, e * chan : (e + 1) * chan
                ]

    spread_left(g, 0)
    partner(0).wait_recv()
    gp = gp_r[...]
    spread_left(gp, 1)

    def arrivals(k):
        r = lax.rem(row + nrow - k, nrow)

        def same():
            copy(f_s.at[1], r_r.at[r], 1, r, r, dev(r, col)).wait_recv()
            copy(f_s.at[0], l_r.at[r], 0, r, r, dev(r, col)).wait_recv()
            copy(m_s, m_r.at[0, r], 4, r, r, dev(r, col)).wait_recv()
            on(
                half_of(row) == col,
                lambda: copy(ct_s.at[0], ct_r.at[r], 3, r, r, dev(r, col)).wait_recv(),
            )

        if isinstance(k, int):
            if k:
                same()
        else:
            on(k != 0, same)
        on(
            half_of(r) == col,
            lambda: copy(f_s.at[1], ro_r.at[r], 2, r, r, dev(r, other)).wait_recv(),
        )
        copy(m_s, m_r.at[1, r], 5, r, r, dev(r, other)).wait_recv()
        on(
            half_of(row) == other,
            lambda: copy(ct_s.at[0], ct_r.at[r], 6, r, r, dev(r, other)).wait_recv(),
        )

    partner(1).wait_recv()
    each(nrow, arrivals)

    rep = (iota((res, nrow), 0) >> lo == iota((res, nrow), 1)).astype(BF16)
    own_lane = (iota((res, 128), 0) & (loc - 1)) == (iota((res, 128), 1) >> sq)
    z = [
        jnp.where(own_lane, mm(rep, m_r[k].reshape(nrow, 128).astype(BF16)), 0.0).astype(BF16)
        for k in range(2)
    ]
    counts = []
    for b in range(loc):
        total = None
        for k, gl in enumerate((g, gp)):
            m_b = jnp.broadcast_to(
                gl[b * seq : (b + 1) * seq, 2 * proj : 2 * proj + 1].astype(F32), (seq, 128)
            ).astype(BF16)
            term = mm(z[k], jnp.concatenate([m_b] * (128 // seq), axis=0))
            total = term if total is None else total + term
        counts.append(jnp.maximum(total, 1.0))

    def unflatten(ref, n, start=0):
        return jnp.concatenate(
            [ref[pl.ds(start + t, n, stride=tiles), :] for t in range(tiles)], axis=1
        ).astype(BF16)

    a32[...] = r_r[...].astype(F32).reshape(res * tiles, 128)
    b32[...] = l_r[...].astype(F32).reshape(res * tiles, 128)
    c32[...] = ct_r[...].astype(F32).reshape(res * loc, 128)
    o32[...] = (
        ro_r[pl.ds(col * per_half, per_half)].astype(F32).reshape(half_res * tiles, 128)
    )
    right_all = unflatten(a32, res)
    left_all = unflatten(b32, res)

    start = pl.multiple_of(col * half_res * tiles, half_res * tiles)
    r_half = jnp.concatenate(
        [unflatten(a32, half_res, start), unflatten(o32, half_res)], axis=1
    )
    mapped = mm(r_half, p2[...])
    bias = bias_ref[...]
    for i in range(loc):
        w32[:res] = counts[i]
        div = w32[pl.ds(pl.multiple_of(col * half_res, half_res), half_res), :]
        pu_ref[i] = (mapped[:, i * chan : (i + 1) * chan] / div + bias).astype(BF16)

    def grad(flat, scaled, weight):
        q = lax.dot_general(
            flat, scaled, (((0,), (0,)), ((), ())), preferred_element_type=F32
        ).astype(BF16)
        for e in range(proj):
            for i in range(loc):
                q2[i * seq : (i + 1) * seq, e * chan : (e + 1) * chan] = q[
                    e * seq : (e + 1) * seq, i * chan : (i + 1) * chan
                ]
        return lax.dot_general(
            q2[...], weight, (((1,), (1,)), ((), ())), preferred_element_type=F32
        )

    scaled = jnp.concatenate(
        [(cf_r[i].astype(F32) / counts[i]).astype(BF16) for i in range(loc)], axis=1
    )
    lg_ref[...] = grad(right_all, scaled, w_c)
    scaled_t = jnp.concatenate(
        [
            (c32[pl.ds(j, res, stride=loc), :] / counts[j]).astype(BF16)
            for j in range(loc)
        ],
        axis=1,
    )
    rg_ref[...] = grad(left_all, scaled_t, w_e)

    partner(0).wait_send()
    partner(1).wait_send()
    each(nrow, lambda j: sends(nrow - 1 - j, lambda d: d.wait_send()))


def per_device(nrow, x, am, rm, wl, wr, w, bias, cot):
    seq, loc, _ = x.shape
    proj = wl.shape[1]
    half_res, chan = cot.shape[1], cot.shape[2]
    res = nrow * loc
    tiles = proj * seq // 128
    fr = loc * tiles
    rows = loc * seq
    vm = pl.BlockSpec(memory_space=pltpu.VMEM)
    pu, lg, rg = pl.pallas_call(
        functools.partial(kernel, nrow),
        out_shape=(
            jax.ShapeDtypeStruct(cot.shape, BF16),
            jax.ShapeDtypeStruct((rows, proj), F32),
            jax.ShapeDtypeStruct((rows, proj), F32),
        ),
        in_specs=[vm] * 8,
        out_specs=(vm, vm, vm),
        scratch_shapes=[
            pltpu.VMEM((rows, 128), BF16),
            pltpu.VMEM((rows, 128), BF16),
            pltpu.VMEM((2, fr, 128), BF16),
            pltpu.VMEM((nrow, fr, 128), BF16),
            pltpu.VMEM((nrow, fr, 128), BF16),
            pltpu.VMEM((nrow, fr, 128), BF16),
            pltpu.VMEM((half_res // loc, loc * loc, 128), BF16),
            pltpu.VMEM((nrow, loc * loc, 128), BF16),
            pltpu.VMEM((loc, res, chan), BF16),
            pltpu.VMEM((1, 128), F32),
            pltpu.VMEM((2, nrow, 1, 128), F32),
            pltpu.VMEM((max(proj * proj, res), chan), F32),
            pltpu.VMEM((res * tiles, 128), F32),
            pltpu.VMEM((res * tiles, 128), F32),
            pltpu.VMEM((half_res * tiles, 128), F32),
            pltpu.VMEM((res * loc, 128), F32),
            pltpu.VMEM((2 * proj * seq, loc * chan), BF16),
            pltpu.VMEM((rows, proj * chan), BF16),
            pltpu.SemaphoreType.DMA((7, nrow)),
            pltpu.SemaphoreType.DMA((7, nrow)),
            pltpu.SemaphoreType.DMA((4,)),
        ],
        compiler_params=pltpu.CompilerParams(collective_id=0, has_side_effects=True),
    )(x, am, rm.reshape(1, loc), wl, wr, w, bias.reshape(1, chan), cot)
    lg = jnp.swapaxes(lg.reshape(loc, seq, proj), 0, 1)
    rg = jnp.swapaxes(rg.reshape(loc, seq, proj), 0, 1)
    return pu, lg, rg


def solution(mesh):
    placed = (
        P(("grp", "col"), "row", None),
        P(("grp", "col"), "row"),
        P(("grp", "row")),
        P(),
        P(),
        P(),
        P(),
        P(("grp", "row"), "col", None),
    )
    return jax.shard_map(
        functools.partial(per_device, mesh.shape["row"]),
        mesh=mesh,
        in_specs=placed,
        out_specs=(
            P(("grp", "row"), "col", None),
            P(("grp", "col"), "row", None),
            P(("grp", "col"), "row", None),
        ),
        check_vma=False,
    )
```

```python
import functools

import jax
import jax.numpy as jnp
from jax import lax
from jax.experimental import pallas as pl
from jax.experimental.pallas import tpu as pltpu
from jax.sharding import PartitionSpec as P

F32 = jnp.float32
BF16 = jnp.bfloat16
MESH = pl.DeviceIdType.MESH
UNROLL = 8


def iota(shape, axis):
    return lax.broadcasted_iota(jnp.int32, shape, axis)


def mm(a, b):
    return lax.dot_general(a, b, (((1,), (0,)), ((), ())), preferred_element_type=F32)


def each(n, f):
    if n <= UNROLL:
        for k in range(n):
            f(k)
    else:

        @pl.loop(0, n)
        def _(k):
            f(k)


def kernel(
    nrow,
    x_hbm, am_hbm, rm_hbm, wl_hbm, wr_hbm, w_hbm, bias_hbm, cot_hbm,
    pu_hbm, lg_hbm, rg_hbm,
    x_ref, am_ref, rm_ref, wl_ref, wr_ref, w_ref, bias_ref, cot_ref,
    pu_ref, lg_ref, rg_ref,
    g_s, gp_r, f_s, l_r, r_r, ro_r, ct_s, ct_r, cf_r, m_s, m_r,
    w32, a32, b32, o32, c32, p2, q2,
    ssem, rsem, psem, isem, osem,
):
    seq, loc, feat = x_ref.shape
    proj = wl_ref.shape[0]
    half_res, chan = cot_ref.shape[1], cot_ref.shape[2]
    res = nrow * loc
    per_half = half_res // loc
    tiles = proj * seq // 128
    rows = loc * seq
    lo = loc.bit_length() - 1
    sq = seq.bit_length() - 1
    tl = tiles.bit_length() - 1

    grp, row, col = lax.axis_index("grp"), lax.axis_index("row"), lax.axis_index("col")
    other = 1 - col

    def half_of(r):
        return jnp.where(r >= per_half, 1, 0)

    def dev(r, c):
        return (grp, r, c)

    barrier = pltpu.get_barrier_semaphore()

    def greet(k):
        r = lax.rem(row + k, nrow)
        pl.semaphore_signal(barrier, inc=1, device_id=dev(r, other), device_id_type=MESH)
        if isinstance(k, int):
            if k:
                pl.semaphore_signal(barrier, inc=1, device_id=dev(r, col), device_id_type=MESH)
        else:

            @pl.when(k != 0)
            def _():
                pl.semaphore_signal(barrier, inc=1, device_id=dev(r, col), device_id_type=MESH)

    each(nrow, greet)
    loads = [
        pltpu.make_async_copy(src, dst, isem.at[k])
        for k, (src, dst) in enumerate(
            (
                (x_hbm, x_ref), (wl_hbm, wl_ref), (wr_hbm, wr_ref), (am_hbm, am_ref),
                (rm_hbm, rm_ref), (cot_hbm, cot_ref), (w_hbm, w_ref), (bias_hbm, bias_ref),
            )
        )
    ]
    for load in loads:
        load.start()
    for load in loads[:6]:
        load.wait()

    xf = x_ref[...].astype(F32)
    x = jnp.concatenate([xf[:, r, :] for r in range(loc)], axis=0).astype(BF16)
    live = jnp.concatenate(
        [
            jnp.broadcast_to(
                (am_ref[r : r + 1, :] * rm_ref[:, r : r + 1]).astype(F32), (seq, seq)
            )
            for r in range(loc)
        ],
        axis=0,
    )
    diagonal = (iota((rows, seq), 0) & (seq - 1)) == iota((rows, seq), 1)
    live = jnp.sum(jnp.where(diagonal, live, 0.0), axis=1, keepdims=True)
    live = jnp.broadcast_to(live, (rows, 128))
    factors = jnp.concatenate(
        [wl_ref[...], wr_ref[...], jnp.zeros((128 - 2 * proj, feat), BF16)], axis=0
    )
    both = lax.dot_general(x, factors, (((1,), (1,)), ((), ())), preferred_element_type=F32)
    both = jnp.where(iota((rows, 128), 1) < 2 * proj, both, 1.0) * live
    g = both.astype(BF16)
    g_s[...] = g
    lane = iota((rows, 128), 1)
    at = iota((rows, 128), 0)
    m_s[...] = jnp.sum(jnp.where(lane == at, live, 0.0), axis=0, keepdims=True)
    width = 2 * proj * seq
    spread = (iota((128, width), 0) == (iota((128, width), 1) >> sq)).astype(BF16)
    own_seq = (iota((rows, width), 0) & (seq - 1)) == (iota((rows, width), 1) & (seq - 1))
    h = jnp.where(own_seq, mm(g, spread), 0.0).astype(BF16)
    h = jnp.concatenate([h[:, k * 128 : (k + 1) * 128] for k in range(2 * tiles)], axis=0)
    frows, deep = 2 * loc * tiles, 2 * tiles * rows
    fi, ki = iota((frows, deep), 0), iota((frows, deep), 1)
    f_x, f_r, f_t = fi >> (lo + tl), (fi >> tl) & (loc - 1), fi & (tiles - 1)
    k_x, k_t, k_r = ki >> (tl + lo + sq), (ki >> (lo + sq)) & (tiles - 1), (ki >> sq) & (loc - 1)
    pick = ((f_x == k_x) & (f_r == k_r) & (f_t == k_t)).astype(BF16)
    f = mm(pick, h).astype(BF16)
    fr = loc * tiles
    f_s[0] = f[:fr]
    f_s[1] = f[fr:]
    cot32 = cot_ref[...].astype(F32)
    for q in range(per_half if per_half <= UNROLL else 0):
        ct_s[q] = jnp.concatenate(
            [cot32[i, q * loc : (q + 1) * loc, :] for i in range(loc)], axis=0
        ).astype(BF16)
    if per_half > UNROLL:
        c32_rows = c32.shape[0] // loc

        for i in range(loc):
            c32[i * c32_rows : i * c32_rows + half_res] = cot32[i]

        @pl.loop(0, per_half)
        def _(q):
            ct_s[q] = jnp.concatenate(
                [
                    c32[pl.ds(i * c32_rows + q * loc, loc), :]
                    for i in range(loc)
                ],
                axis=0,
            ).astype(BF16)

    pl.semaphore_wait(barrier, 2 * nrow - 1)

    def copy(src, dst, kind, s_slot, r_slot, to):
        return pltpu.make_async_remote_copy(
            src_ref=src, dst_ref=dst, send_sem=ssem.at[kind, s_slot],
            recv_sem=rsem.at[kind, r_slot], device_id=to, device_id_type=MESH,
        )

    def partner(k):
        if k == 0:
            src, dst = g_s, gp_r
        else:
            src, dst = cot_ref, cf_r.at[:, pl.ds(pl.multiple_of(col * half_res, half_res), half_res), :]
        return pltpu.make_async_remote_copy(
            src_ref=src, dst_ref=dst, send_sem=psem.at[k], recv_sem=psem.at[2 + k],
            device_id=dev(row, other), device_id_type=MESH,
        )

    def on(pred, f):
        pl.when(pred)(f)

    def sends(k, act):
        r = lax.rem(row + k, nrow)
        q = jnp.where(r >= per_half, r - per_half, r)
        far = half_of(r) == col

        def same():
            act(copy(f_s.at[1], r_r.at[row], 1, r, row, dev(r, col)))
            act(copy(f_s.at[0], l_r.at[row], 0, r, row, dev(r, col)))
            act(copy(m_s, m_r.at[0, row], 4, r, row, dev(r, col)))
            on(far, lambda: act(copy(ct_s.at[q], ct_r.at[row], 3, r, row, dev(r, col))))

        if isinstance(k, int):
            if k:
                same()
        else:
            on(k != 0, same)
        on(
            half_of(row) == other,
            lambda: act(copy(f_s.at[1], ro_r.at[row], 2, r, row, dev(r, other))),
        )
        act(copy(m_s, m_r.at[1, row], 5, r, row, dev(r, other)))
        on(far, lambda: act(copy(ct_s.at[q], ct_r.at[row], 6, r, row, dev(r, other))))

    partner(0).start()
    partner(1).start()
    each(nrow, lambda j: sends(nrow - 1 - j, lambda d: d.start()))

    l_r[row] = f[:fr]
    r_r[row] = f[fr:]
    m_r[0, row] = m_s[...]
    cf_r[:, pl.ds(pl.multiple_of(col * half_res, half_res), half_res), :] = cot_ref[...]

    @pl.when(half_of(row) == col)
    def _():
        ct_r[row] = ct_s[jnp.where(row >= per_half, row - per_half, row)]

    loads[6].wait()
    loads[7].wait()
    w32[...] = w_ref[...].astype(F32)
    w_c = jnp.concatenate(
        [w32[pl.ds(e, proj, stride=proj), :] for e in range(proj)], axis=1
    ).astype(BF16)
    w_e = jnp.concatenate(
        [w_ref[c * proj : (c + 1) * proj, :] for c in range(proj)], axis=1
    )

    def spread_left(gl, part):
        p = mm(gl[:, :proj], w_c).astype(BF16)
        for e in range(proj):
            for i in range(loc):
                p2[part * proj * seq + e * seq : part * proj * seq + (e + 1) * seq,
                   i * chan : (i + 1) * chan] = p[
                    i * seq : (i + 1) * seq, e * chan : (e + 1) * chan
                ]

    spread_left(g, 0)
    partner(0).wait_recv()
    gp = gp_r[...]
    spread_left(gp, 1)

    def arrivals(k):
        r = lax.rem(row + nrow - k, nrow)

        def same():
            copy(f_s.at[1], r_r.at[r], 1, r, r, dev(r, col)).wait_recv()
            copy(f_s.at[0], l_r.at[r], 0, r, r, dev(r, col)).wait_recv()
            copy(m_s, m_r.at[0, r], 4, r, r, dev(r, col)).wait_recv()
            on(
                half_of(row) == col,
                lambda: copy(ct_s.at[0], ct_r.at[r], 3, r, r, dev(r, col)).wait_recv(),
            )

        if isinstance(k, int):
            if k:
                same()
        else:
            on(k != 0, same)
        on(
            half_of(r) == col,
            lambda: copy(f_s.at[1], ro_r.at[r], 2, r, r, dev(r, other)).wait_recv(),
        )
        copy(m_s, m_r.at[1, r], 5, r, r, dev(r, other)).wait_recv()
        on(
            half_of(row) == other,
            lambda: copy(ct_s.at[0], ct_r.at[r], 6, r, r, dev(r, other)).wait_recv(),
        )

    partner(1).wait_recv()
    each(nrow, arrivals)

    rep = (iota((res, nrow), 0) >> lo == iota((res, nrow), 1)).astype(BF16)
    own_lane = (iota((res, 128), 0) & (loc - 1)) == (iota((res, 128), 1) >> sq)
    z = [
        jnp.where(own_lane, mm(rep, m_r[k].reshape(nrow, 128).astype(BF16)), 0.0).astype(BF16)
        for k in range(2)
    ]
    counts = []
    for b in range(loc):
        total = None
        for k, gl in enumerate((g, gp)):
            m_b = jnp.broadcast_to(
                gl[b * seq : (b + 1) * seq, 2 * proj : 2 * proj + 1].astype(F32), (seq, 128)
            ).astype(BF16)
            term = mm(z[k], jnp.concatenate([m_b] * (128 // seq), axis=0))
            total = term if total is None else total + term
        counts.append(jnp.maximum(total, 1.0))

    def unflatten(ref, n, start=0):
        return jnp.concatenate(
            [ref[pl.ds(start + t, n, stride=tiles), :] for t in range(tiles)], axis=1
        ).astype(BF16)

    a32[...] = r_r[...].astype(F32).reshape(res * tiles, 128)
    b32[...] = l_r[...].astype(F32).reshape(res * tiles, 128)
    c32[...] = ct_r[...].astype(F32).reshape(res * loc, 128)
    o32[...] = (
        ro_r[pl.ds(col * per_half, per_half)].astype(F32).reshape(half_res * tiles, 128)
    )
    right_all = unflatten(a32, res)
    left_all = unflatten(b32, res)

    start = pl.multiple_of(col * half_res * tiles, half_res * tiles)
    r_half = jnp.concatenate(
        [unflatten(a32, half_res, start), unflatten(o32, half_res)], axis=1
    )
    mapped = mm(r_half, p2[...])
    bias = bias_ref[...]
    for i in range(loc):
        w32[:res] = counts[i]
        div = w32[pl.ds(pl.multiple_of(col * half_res, half_res), half_res), :]
        pu_ref[i] = (mapped[:, i * chan : (i + 1) * chan] / div + bias).astype(BF16)

    stores = [
        pltpu.make_async_copy(src, dst, osem.at[k])
        for k, (src, dst) in enumerate(((pu_ref, pu_hbm), (lg_ref, lg_hbm), (rg_ref, rg_hbm)))
    ]
    stores[0].start()

    def grad(flat, scaled, weight):
        q = lax.dot_general(
            flat, scaled, (((0,), (0,)), ((), ())), preferred_element_type=F32
        ).astype(BF16)
        for e in range(proj):
            for i in range(loc):
                q2[i * seq : (i + 1) * seq, e * chan : (e + 1) * chan] = q[
                    e * seq : (e + 1) * seq, i * chan : (i + 1) * chan
                ]
        return lax.dot_general(
            q2[...], weight, (((1,), (1,)), ((), ())), preferred_element_type=F32
        )

    scaled = jnp.concatenate(
        [(cf_r[i].astype(F32) / counts[i]).astype(BF16) for i in range(loc)], axis=1
    )
    lg_ref[...] = grad(right_all, scaled, w_c)
    stores[1].start()
    scaled_t = jnp.concatenate(
        [
            (c32[pl.ds(j, res, stride=loc), :] / counts[j]).astype(BF16)
            for j in range(loc)
        ],
        axis=1,
    )
    rg_ref[...] = grad(left_all, scaled_t, w_e)
    stores[2].start()

    partner(0).wait_send()
    partner(1).wait_send()
    each(nrow, lambda j: sends(nrow - 1 - j, lambda d: d.wait_send()))
    for store in stores:
        store.wait()


def per_device(nrow, x, am, rm, wl, wr, w, bias, cot):
    seq, loc, _ = x.shape
    proj = wl.shape[1]
    half_res, chan = cot.shape[1], cot.shape[2]
    res = nrow * loc
    tiles = proj * seq // 128
    fr = loc * tiles
    rows = loc * seq
    hbm = pl.BlockSpec(memory_space=pl.ANY)
    operands = (x, am.T, rm.reshape(1, loc), wl.T, wr.T, w, bias.reshape(1, chan), cot)
    pu, lg, rg = pl.pallas_call(
        functools.partial(kernel, nrow),
        out_shape=(
            jax.ShapeDtypeStruct(cot.shape, BF16),
            jax.ShapeDtypeStruct((rows, proj), F32),
            jax.ShapeDtypeStruct((rows, proj), F32),
        ),
        in_specs=[hbm] * 8,
        out_specs=(hbm, hbm, hbm),
        scratch_shapes=[pltpu.VMEM(a.shape, a.dtype) for a in operands]
        + [
            pltpu.VMEM(cot.shape, BF16),
            pltpu.VMEM((rows, proj), F32),
            pltpu.VMEM((rows, proj), F32),
            pltpu.VMEM((rows, 128), BF16),
            pltpu.VMEM((rows, 128), BF16),
            pltpu.VMEM((2, fr, 128), BF16),
            pltpu.VMEM((nrow, fr, 128), BF16),
            pltpu.VMEM((nrow, fr, 128), BF16),
            pltpu.VMEM((nrow, fr, 128), BF16),
            pltpu.VMEM((half_res // loc, loc * loc, 128), BF16),
            pltpu.VMEM((nrow, loc * loc, 128), BF16),
            pltpu.VMEM((loc, res, chan), BF16),
            pltpu.VMEM((1, 128), F32),
            pltpu.VMEM((2, nrow, 1, 128), F32),
            pltpu.VMEM((max(proj * proj, res), chan), F32),
            pltpu.VMEM((res * tiles, 128), F32),
            pltpu.VMEM((res * tiles, 128), F32),
            pltpu.VMEM((half_res * tiles, 128), F32),
            pltpu.VMEM((res * loc, 128), F32),
            pltpu.VMEM((2 * proj * seq, loc * chan), BF16),
            pltpu.VMEM((rows, proj * chan), BF16),
            pltpu.SemaphoreType.DMA((7, nrow)),
            pltpu.SemaphoreType.DMA((7, nrow)),
            pltpu.SemaphoreType.DMA((4,)),
            pltpu.SemaphoreType.DMA((8,)),
            pltpu.SemaphoreType.DMA((3,)),
        ],
        compiler_params=pltpu.CompilerParams(collective_id=0, has_side_effects=True),
    )(*operands)
    lg = jnp.swapaxes(lg.reshape(loc, seq, proj), 0, 1)
    rg = jnp.swapaxes(rg.reshape(loc, seq, proj), 0, 1)
    return pu, lg, rg


def solution(mesh):
    placed = (
        P(("grp", "col"), "row", None),
        P(("grp", "col"), "row"),
        P(("grp", "row")),
        P(),
        P(),
        P(),
        P(),
        P(("grp", "row"), "col", None),
    )
    return jax.shard_map(
        functools.partial(per_device, mesh.shape["row"]),
        mesh=mesh,
        in_specs=placed,
        out_specs=(
            P(("grp", "row"), "col", None),
            P(("grp", "col"), "row", None),
            P(("grp", "col"), "row", None),
        ),
        check_vma=False,
    )
```

```python
import functools

import jax
import jax.numpy as jnp
from jax import lax
from jax.experimental import pallas as pl
from jax.experimental.pallas import tpu as pltpu
from jax.sharding import PartitionSpec as P

F32 = jnp.float32
BF16 = jnp.bfloat16
MESH = pl.DeviceIdType.MESH
UNROLL = 8
GRANT = 24 << 20


def iota(shape, axis):
    return lax.broadcasted_iota(jnp.int32, shape, axis)


def mm(a, b):
    return lax.dot_general(a, b, (((1,), (0,)), ((), ())), preferred_element_type=F32)


def each(n, f):
    if n <= UNROLL:
        for k in range(n):
            f(k)
    else:

        @pl.loop(0, n)
        def _(k):
            f(k)


def kernel(
    nrow,
    x_hbm, am_hbm, rm_hbm, wl_hbm, wr_hbm, w_hbm, bias_hbm, cot_hbm,
    pu_ref, lg_ref, rg_ref,
    x_ref, am_ref, rm_ref, wl_ref, wr_ref, w_ref, bias_ref, cot_ref,
    g_s, gp_r, f_s, l_r, r_r, ro_r, ct_s, ct_r, cf_r, m_s, m_r,
    w32, a32, b32, o32, c32, p2, q2,
    ssem, rsem, psem, isem,
):
    seq, loc, feat = x_ref.shape
    proj = wl_ref.shape[0]
    half_res, chan = cot_ref.shape[1], cot_ref.shape[2]
    res = nrow * loc
    per_half = half_res // loc
    tiles = proj * seq // 128
    rows = loc * seq
    lo = loc.bit_length() - 1
    sq = seq.bit_length() - 1
    tl = tiles.bit_length() - 1

    grp, row, col = lax.axis_index("grp"), lax.axis_index("row"), lax.axis_index("col")
    other = 1 - col

    def half_of(r):
        return jnp.where(r >= per_half, 1, 0)

    def dev(r, c):
        return (grp, r, c)

    barrier = pltpu.get_barrier_semaphore()

    def greet(k):
        r = lax.rem(row + k, nrow)
        pl.semaphore_signal(barrier, inc=1, device_id=dev(r, other), device_id_type=MESH)
        if isinstance(k, int):
            if k:
                pl.semaphore_signal(barrier, inc=1, device_id=dev(r, col), device_id_type=MESH)
        else:

            @pl.when(k != 0)
            def _():
                pl.semaphore_signal(barrier, inc=1, device_id=dev(r, col), device_id_type=MESH)

    each(nrow, greet)
    loads = [
        pltpu.make_async_copy(src, dst, isem.at[k])
        for k, (src, dst) in enumerate(
            (
                (x_hbm, x_ref), (wl_hbm, wl_ref), (wr_hbm, wr_ref), (am_hbm, am_ref),
                (rm_hbm, rm_ref), (cot_hbm, cot_ref), (w_hbm, w_ref), (bias_hbm, bias_ref),
            )
        )
    ]
    for load in loads:
        load.start()
    for load in loads[:6]:
        load.wait()

    xf = x_ref[...].astype(F32)
    x = jnp.concatenate([xf[:, r, :] for r in range(loc)], axis=0).astype(BF16)
    live = jnp.concatenate(
        [
            jnp.broadcast_to(
                (am_ref[r : r + 1, :] * rm_ref[:, r : r + 1]).astype(F32), (seq, seq)
            )
            for r in range(loc)
        ],
        axis=0,
    )
    diagonal = (iota((rows, seq), 0) & (seq - 1)) == iota((rows, seq), 1)
    live = jnp.sum(jnp.where(diagonal, live, 0.0), axis=1, keepdims=True)
    live = jnp.broadcast_to(live, (rows, 128))
    factors = jnp.concatenate(
        [wl_ref[...], wr_ref[...], jnp.zeros((128 - 2 * proj, feat), BF16)], axis=0
    )
    both = lax.dot_general(x, factors, (((1,), (1,)), ((), ())), preferred_element_type=F32)
    both = jnp.where(iota((rows, 128), 1) < 2 * proj, both, 1.0) * live
    g = both.astype(BF16)
    g_s[...] = g
    lane = iota((rows, 128), 1)
    at = iota((rows, 128), 0)
    m_s[...] = jnp.sum(jnp.where(lane == at, live, 0.0), axis=0, keepdims=True)
    width = 2 * proj * seq
    spread = (iota((128, width), 0) == (iota((128, width), 1) >> sq)).astype(BF16)
    own_seq = (iota((rows, width), 0) & (seq - 1)) == (iota((rows, width), 1) & (seq - 1))
    h = jnp.where(own_seq, mm(g, spread), 0.0).astype(BF16)
    h = jnp.concatenate([h[:, k * 128 : (k + 1) * 128] for k in range(2 * tiles)], axis=0)
    frows, deep = 2 * loc * tiles, 2 * tiles * rows
    fi, ki = iota((frows, deep), 0), iota((frows, deep), 1)
    f_x, f_r, f_t = fi >> (lo + tl), (fi >> tl) & (loc - 1), fi & (tiles - 1)
    k_x, k_t, k_r = ki >> (tl + lo + sq), (ki >> (lo + sq)) & (tiles - 1), (ki >> sq) & (loc - 1)
    pick = ((f_x == k_x) & (f_r == k_r) & (f_t == k_t)).astype(BF16)
    f = mm(pick, h).astype(BF16)
    fr = loc * tiles
    f_s[0] = f[:fr]
    f_s[1] = f[fr:]
    cot32 = cot_ref[...].astype(F32)
    for q in range(per_half if per_half <= UNROLL else 0):
        ct_s[q] = jnp.concatenate(
            [cot32[i, q * loc : (q + 1) * loc, :] for i in range(loc)], axis=0
        ).astype(BF16)
    if per_half > UNROLL:
        c32_rows = c32.shape[0] // loc

        for i in range(loc):
            c32[i * c32_rows : i * c32_rows + half_res] = cot32[i]

        @pl.loop(0, per_half)
        def _(q):
            ct_s[q] = jnp.concatenate(
                [
                    c32[pl.ds(i * c32_rows + q * loc, loc), :]
                    for i in range(loc)
                ],
                axis=0,
            ).astype(BF16)

    pl.semaphore_wait(barrier, 2 * nrow - 1)

    def copy(src, dst, kind, s_slot, r_slot, to):
        return pltpu.make_async_remote_copy(
            src_ref=src, dst_ref=dst, send_sem=ssem.at[kind, s_slot],
            recv_sem=rsem.at[kind, r_slot], device_id=to, device_id_type=MESH,
        )

    def partner(k):
        if k == 0:
            src, dst = g_s, gp_r
        else:
            src, dst = cot_ref, cf_r.at[:, pl.ds(pl.multiple_of(col * half_res, half_res), half_res), :]
        return pltpu.make_async_remote_copy(
            src_ref=src, dst_ref=dst, send_sem=psem.at[k], recv_sem=psem.at[2 + k],
            device_id=dev(row, other), device_id_type=MESH,
        )

    def on(pred, f):
        pl.when(pred)(f)

    def sends(k, act):
        r = lax.rem(row + k, nrow)
        q = jnp.where(r >= per_half, r - per_half, r)
        far = half_of(r) == col

        def same():
            act(copy(f_s.at[1], r_r.at[row], 1, r, row, dev(r, col)))
            act(copy(f_s.at[0], l_r.at[row], 0, r, row, dev(r, col)))
            act(copy(m_s, m_r.at[0, row], 4, r, row, dev(r, col)))
            on(far, lambda: act(copy(ct_s.at[q], ct_r.at[row], 3, r, row, dev(r, col))))

        if isinstance(k, int):
            if k:
                same()
        else:
            on(k != 0, same)
        on(
            half_of(row) == other,
            lambda: act(copy(f_s.at[1], ro_r.at[row], 2, r, row, dev(r, other))),
        )
        act(copy(m_s, m_r.at[1, row], 5, r, row, dev(r, other)))
        on(far, lambda: act(copy(ct_s.at[q], ct_r.at[row], 6, r, row, dev(r, other))))

    partner(0).start()
    partner(1).start()
    each(nrow, lambda j: sends(nrow - 1 - j, lambda d: d.start()))

    l_r[row] = f[:fr]
    r_r[row] = f[fr:]
    m_r[0, row] = m_s[...]
    cf_r[:, pl.ds(pl.multiple_of(col * half_res, half_res), half_res), :] = cot_ref[...]

    @pl.when(half_of(row) == col)
    def _():
        ct_r[row] = ct_s[jnp.where(row >= per_half, row - per_half, row)]

    loads[6].wait()
    loads[7].wait()
    w32[...] = w_ref[...].astype(F32)
    w_c = jnp.concatenate(
        [w32[pl.ds(e, proj, stride=proj), :] for e in range(proj)], axis=1
    ).astype(BF16)
    w_e = jnp.concatenate(
        [w_ref[c * proj : (c + 1) * proj, :] for c in range(proj)], axis=1
    )

    def spread_left(gl, part):
        p = mm(gl[:, :proj], w_c).astype(BF16)
        for e in range(proj):
            for i in range(loc):
                p2[part * proj * seq + e * seq : part * proj * seq + (e + 1) * seq,
                   i * chan : (i + 1) * chan] = p[
                    i * seq : (i + 1) * seq, e * chan : (e + 1) * chan
                ]

    spread_left(g, 0)
    partner(0).wait_recv()
    gp = gp_r[...]
    spread_left(gp, 1)

    def arrivals(k):
        r = lax.rem(row + nrow - k, nrow)

        def same():
            copy(f_s.at[1], r_r.at[r], 1, r, r, dev(r, col)).wait_recv()
            copy(f_s.at[0], l_r.at[r], 0, r, r, dev(r, col)).wait_recv()
            copy(m_s, m_r.at[0, r], 4, r, r, dev(r, col)).wait_recv()
            on(
                half_of(row) == col,
                lambda: copy(ct_s.at[0], ct_r.at[r], 3, r, r, dev(r, col)).wait_recv(),
            )

        if isinstance(k, int):
            if k:
                same()
        else:
            on(k != 0, same)
        on(
            half_of(r) == col,
            lambda: copy(f_s.at[1], ro_r.at[r], 2, r, r, dev(r, other)).wait_recv(),
        )
        copy(m_s, m_r.at[1, r], 5, r, r, dev(r, other)).wait_recv()
        on(
            half_of(row) == other,
            lambda: copy(ct_s.at[0], ct_r.at[r], 6, r, r, dev(r, other)).wait_recv(),
        )

    partner(1).wait_recv()
    each(nrow, arrivals)

    rep = (iota((res, nrow), 0) >> lo == iota((res, nrow), 1)).astype(BF16)
    own_lane = (iota((res, 128), 0) & (loc - 1)) == (iota((res, 128), 1) >> sq)
    z = [
        jnp.where(own_lane, mm(rep, m_r[k].reshape(nrow, 128).astype(BF16)), 0.0).astype(BF16)
        for k in range(2)
    ]
    counts = []
    for b in range(loc):
        total = None
        for k, gl in enumerate((g, gp)):
            m_b = jnp.broadcast_to(
                gl[b * seq : (b + 1) * seq, 2 * proj : 2 * proj + 1].astype(F32), (seq, 128)
            ).astype(BF16)
            term = mm(z[k], jnp.concatenate([m_b] * (128 // seq), axis=0))
            total = term if total is None else total + term
        counts.append(jnp.maximum(total, 1.0))

    def unflatten(ref, n, start=0):
        return jnp.concatenate(
            [ref[pl.ds(start + t, n, stride=tiles), :] for t in range(tiles)], axis=1
        ).astype(BF16)

    a32[...] = r_r[...].astype(F32).reshape(res * tiles, 128)
    b32[...] = l_r[...].astype(F32).reshape(res * tiles, 128)
    c32[...] = ct_r[...].astype(F32).reshape(res * loc, 128)
    o32[...] = (
        ro_r[pl.ds(col * per_half, per_half)].astype(F32).reshape(half_res * tiles, 128)
    )
    right_all = unflatten(a32, res)
    left_all = unflatten(b32, res)

    start = pl.multiple_of(col * half_res * tiles, half_res * tiles)
    r_half = jnp.concatenate(
        [unflatten(a32, half_res, start), unflatten(o32, half_res)], axis=1
    )
    mapped = mm(r_half, p2[...])
    bias = bias_ref[...]
    for i in range(loc):
        w32[:res] = counts[i]
        div = w32[pl.ds(pl.multiple_of(col * half_res, half_res), half_res), :]
        pu_ref[i] = (mapped[:, i * chan : (i + 1) * chan] / div + bias).astype(BF16)

    def grad(flat, scaled, weight):
        q = lax.dot_general(
            flat, scaled, (((0,), (0,)), ((), ())), preferred_element_type=F32
        ).astype(BF16)
        for e in range(proj):
            for i in range(loc):
                q2[i * seq : (i + 1) * seq, e * chan : (e + 1) * chan] = q[
                    e * seq : (e + 1) * seq, i * chan : (i + 1) * chan
                ]
        return lax.dot_general(
            q2[...], weight, (((1,), (1,)), ((), ())), preferred_element_type=F32
        )

    scaled = jnp.concatenate(
        [(cf_r[i].astype(F32) / counts[i]).astype(BF16) for i in range(loc)], axis=1
    )
    lg_ref[...] = grad(right_all, scaled, w_c)
    scaled_t = jnp.concatenate(
        [
            (c32[pl.ds(j, res, stride=loc), :] / counts[j]).astype(BF16)
            for j in range(loc)
        ],
        axis=1,
    )
    rg_ref[...] = grad(left_all, scaled_t, w_e)

    partner(0).wait_send()
    partner(1).wait_send()
    each(nrow, lambda j: sends(nrow - 1 - j, lambda d: d.wait_send()))


def finish(pu_in, lg_in, rg_in, pu_ref, lg_ref, rg_ref):
    seq, loc, _ = lg_ref.shape
    pu_ref[...] = pu_in[...]
    for i in range(loc):
        lg_ref[:, i, :] = lg_in[i * seq : (i + 1) * seq, :]
        rg_ref[:, i, :] = rg_in[i * seq : (i + 1) * seq, :]


def per_device(nrow, x, am, rm, wl, wr, w, bias, cot):
    seq, loc, _ = x.shape
    proj = wl.shape[1]
    half_res, chan = cot.shape[1], cot.shape[2]
    res = nrow * loc
    tiles = proj * seq // 128
    fr = loc * tiles
    rows = loc * seq
    hbm = pl.BlockSpec(memory_space=pltpu.HBM)
    vm = pl.BlockSpec(memory_space=pltpu.VMEM)
    operands = (x, am.T, rm.reshape(1, loc), wl.T, wr.T, w, bias.reshape(1, chan), cot)
    pu, lg, rg = pl.pallas_call(
        functools.partial(kernel, nrow),
        out_shape=(
            jax.ShapeDtypeStruct(cot.shape, BF16),
            jax.ShapeDtypeStruct((rows, proj), F32),
            jax.ShapeDtypeStruct((rows, proj), F32),
        ),
        in_specs=[hbm] * 8,
        out_specs=(vm, vm, vm),
        scratch_shapes=[pltpu.VMEM(a.shape, a.dtype) for a in operands]
        + [
            pltpu.VMEM((rows, 128), BF16),
            pltpu.VMEM((rows, 128), BF16),
            pltpu.VMEM((2, fr, 128), BF16),
            pltpu.VMEM((nrow, fr, 128), BF16),
            pltpu.VMEM((nrow, fr, 128), BF16),
            pltpu.VMEM((nrow, fr, 128), BF16),
            pltpu.VMEM((half_res // loc, loc * loc, 128), BF16),
            pltpu.VMEM((nrow, loc * loc, 128), BF16),
            pltpu.VMEM((loc, res, chan), BF16),
            pltpu.VMEM((1, 128), F32),
            pltpu.VMEM((2, nrow, 1, 128), F32),
            pltpu.VMEM((max(proj * proj, res), chan), F32),
            pltpu.VMEM((res * tiles, 128), F32),
            pltpu.VMEM((res * tiles, 128), F32),
            pltpu.VMEM((half_res * tiles, 128), F32),
            pltpu.VMEM((res * loc, 128), F32),
            pltpu.VMEM((2 * proj * seq, loc * chan), BF16),
            pltpu.VMEM((rows, proj * chan), BF16),
            pltpu.SemaphoreType.DMA((7, nrow)),
            pltpu.SemaphoreType.DMA((7, nrow)),
            pltpu.SemaphoreType.DMA((4,)),
            pltpu.SemaphoreType.DMA((8,)),
        ],
        compiler_params=pltpu.CompilerParams(
            collective_id=0, has_side_effects=True, vmem_limit_bytes=GRANT
        ),
    )(*operands)
    grads = jax.ShapeDtypeStruct((seq, loc, proj), F32)
    return pl.pallas_call(
        finish,
        out_shape=(jax.ShapeDtypeStruct(cot.shape, BF16), grads, grads),
        in_specs=[vm] * 3,
        out_specs=(vm, vm, vm),
        compiler_params=pltpu.CompilerParams(vmem_limit_bytes=GRANT),
    )(pu, lg, rg)


def solution(mesh):
    placed = (
        P(("grp", "col"), "row", None),
        P(("grp", "col"), "row"),
        P(("grp", "row")),
        P(),
        P(),
        P(),
        P(),
        P(("grp", "row"), "col", None),
    )
    return jax.shard_map(
        functools.partial(per_device, mesh.shape["row"]),
        mesh=mesh,
        in_specs=placed,
        out_specs=(
            P(("grp", "row"), "col", None),
            P(("grp", "col"), "row", None),
            P(("grp", "col"), "row", None),
        ),
        check_vma=False,
    )
```

```python
import functools

import jax
import jax.numpy as jnp
from jax import lax
from jax.experimental import pallas as pl
from jax.experimental.pallas import tpu as pltpu
from jax.sharding import PartitionSpec as P

F32 = jnp.float32
BF16 = jnp.bfloat16
MESH = pl.DeviceIdType.MESH
UNROLL = 8
GRANT = 24 << 20


def iota(shape, axis):
    return lax.broadcasted_iota(jnp.int32, shape, axis)


def mm(a, b):
    return lax.dot_general(a, b, (((1,), (0,)), ((), ())), preferred_element_type=F32)


def each(n, f):
    if n <= UNROLL:
        for k in range(n):
            f(k)
    else:

        @pl.loop(0, n)
        def _(k):
            f(k)


def kernel(
    nrow,
    x_hbm, am_hbm, rm_hbm, wl_hbm, wr_hbm, w_hbm, bias_hbm, cot_hbm,
    pu_ref, lg_ref, rg_ref,
    x_ref, am_ref, rm_ref, wl_ref, wr_ref, w_ref, bias_ref, cot_ref,
    g_s, gp_r, f_s, l_r, r_r, ro_r, ct_s, ct_r, cf_r, m_s, m_r,
    w32, a32, b32, o32, c32, p2, q2,
    ssem, rsem, psem, isem,
):
    seq, loc, feat = x_ref.shape
    proj = wl_ref.shape[0]
    half_res, chan = cot_ref.shape[1], cot_ref.shape[2]
    res = nrow * loc
    per_half = half_res // loc
    tiles = proj * seq // 128
    rows = loc * seq
    lo = loc.bit_length() - 1
    sq = seq.bit_length() - 1
    tl = tiles.bit_length() - 1

    grp, row, col = lax.axis_index("grp"), lax.axis_index("row"), lax.axis_index("col")
    other = 1 - col

    def half_of(r):
        return jnp.where(r >= per_half, 1, 0)

    def dev(r, c):
        return (grp, r, c)

    barrier = pltpu.get_barrier_semaphore()

    def greet(k):
        r = lax.rem(row + k, nrow)
        pl.semaphore_signal(barrier, inc=1, device_id=dev(r, other), device_id_type=MESH)
        if isinstance(k, int):
            if k:
                pl.semaphore_signal(barrier, inc=1, device_id=dev(r, col), device_id_type=MESH)
        else:

            @pl.when(k != 0)
            def _():
                pl.semaphore_signal(barrier, inc=1, device_id=dev(r, col), device_id_type=MESH)

    each(nrow, greet)
    loads = [
        pltpu.make_async_copy(src, dst, isem.at[k])
        for k, (src, dst) in enumerate(
            (
                (x_hbm, x_ref), (wl_hbm, wl_ref), (wr_hbm, wr_ref), (am_hbm, am_ref),
                (rm_hbm, rm_ref), (cot_hbm, cot_ref), (w_hbm, w_ref), (bias_hbm, bias_ref),
            )
        )
    ]
    for load in loads:
        load.start()
    for load in loads[:6]:
        load.wait()

    xf = x_ref[...].astype(F32)
    x = jnp.concatenate([xf[:, r, :] for r in range(loc)], axis=0).astype(BF16)
    live = jnp.concatenate(
        [
            jnp.broadcast_to(
                (am_ref[r : r + 1, :] * rm_ref[:, r : r + 1]).astype(F32), (seq, seq)
            )
            for r in range(loc)
        ],
        axis=0,
    )
    diagonal = (iota((rows, seq), 0) & (seq - 1)) == iota((rows, seq), 1)
    live = jnp.sum(jnp.where(diagonal, live, 0.0), axis=1, keepdims=True)
    live = jnp.broadcast_to(live, (rows, 128))
    factors = jnp.concatenate(
        [wl_ref[...], wr_ref[...], jnp.zeros((128 - 2 * proj, feat), BF16)], axis=0
    )
    both = lax.dot_general(x, factors, (((1,), (1,)), ((), ())), preferred_element_type=F32)
    both = jnp.where(iota((rows, 128), 1) < 2 * proj, both, 1.0) * live
    g = both.astype(BF16)
    g_s[...] = g
    lane = iota((rows, 128), 1)
    at = iota((rows, 128), 0)
    m_s[...] = jnp.sum(jnp.where(lane == at, live, 0.0), axis=0, keepdims=True)
    width = 2 * proj * seq
    spread = (iota((128, width), 0) == (iota((128, width), 1) >> sq)).astype(BF16)
    own_seq = (iota((rows, width), 0) & (seq - 1)) == (iota((rows, width), 1) & (seq - 1))
    h = jnp.where(own_seq, mm(g, spread), 0.0).astype(BF16)
    h = jnp.concatenate([h[:, k * 128 : (k + 1) * 128] for k in range(2 * tiles)], axis=0)
    frows, deep = 2 * loc * tiles, 2 * tiles * rows
    fi, ki = iota((frows, deep), 0), iota((frows, deep), 1)
    f_x, f_r, f_t = fi >> (lo + tl), (fi >> tl) & (loc - 1), fi & (tiles - 1)
    k_x, k_t, k_r = ki >> (tl + lo + sq), (ki >> (lo + sq)) & (tiles - 1), (ki >> sq) & (loc - 1)
    pick = ((f_x == k_x) & (f_r == k_r) & (f_t == k_t)).astype(BF16)
    f = mm(pick, h).astype(BF16)
    fr = loc * tiles
    f_s[0] = f[:fr]
    f_s[1] = f[fr:]
    cot32 = cot_ref[...].astype(F32)
    for q in range(per_half if per_half <= UNROLL else 0):
        ct_s[q] = jnp.concatenate(
            [cot32[i, q * loc : (q + 1) * loc, :] for i in range(loc)], axis=0
        ).astype(BF16)
    if per_half > UNROLL:
        c32_rows = c32.shape[0] // loc

        for i in range(loc):
            c32[i * c32_rows : i * c32_rows + half_res] = cot32[i]

        @pl.loop(0, per_half)
        def _(q):
            ct_s[q] = jnp.concatenate(
                [
                    c32[pl.ds(i * c32_rows + q * loc, loc), :]
                    for i in range(loc)
                ],
                axis=0,
            ).astype(BF16)

    pl.semaphore_wait(barrier, 2 * nrow - 1)

    def copy(src, dst, kind, s_slot, r_slot, to):
        return pltpu.make_async_remote_copy(
            src_ref=src, dst_ref=dst, send_sem=ssem.at[kind, s_slot],
            recv_sem=rsem.at[kind, r_slot], device_id=to, device_id_type=MESH,
        )

    def partner(k):
        if k == 0:
            src, dst = g_s, gp_r
        else:
            src, dst = cot_ref, cf_r.at[:, pl.ds(pl.multiple_of(col * half_res, half_res), half_res), :]
        return pltpu.make_async_remote_copy(
            src_ref=src, dst_ref=dst, send_sem=psem.at[k], recv_sem=psem.at[2 + k],
            device_id=dev(row, other), device_id_type=MESH,
        )

    def on(pred, f):
        pl.when(pred)(f)

    def sends(k, act):
        r = lax.rem(row + k, nrow)
        q = jnp.where(r >= per_half, r - per_half, r)
        far = half_of(r) == col

        def same():
            act(copy(f_s.at[1], r_r.at[row], 1, r, row, dev(r, col)))
            act(copy(f_s.at[0], l_r.at[row], 0, r, row, dev(r, col)))
            act(copy(m_s, m_r.at[0, row], 4, r, row, dev(r, col)))
            on(far, lambda: act(copy(ct_s.at[q], ct_r.at[row], 3, r, row, dev(r, col))))

        if isinstance(k, int):
            if k:
                same()
        else:
            on(k != 0, same)
        on(
            half_of(row) == other,
            lambda: act(copy(f_s.at[1], ro_r.at[row], 2, r, row, dev(r, other))),
        )
        act(copy(m_s, m_r.at[1, row], 5, r, row, dev(r, other)))
        on(far, lambda: act(copy(ct_s.at[q], ct_r.at[row], 6, r, row, dev(r, other))))

    partner(0).start()
    partner(1).start()
    each(nrow, lambda j: sends(nrow - 1 - j, lambda d: d.start()))

    l_r[row] = f[:fr]
    r_r[row] = f[fr:]
    m_r[0, row] = m_s[...]
    cf_r[:, pl.ds(pl.multiple_of(col * half_res, half_res), half_res), :] = cot_ref[...]

    @pl.when(half_of(row) == col)
    def _():
        ct_r[row] = ct_s[jnp.where(row >= per_half, row - per_half, row)]

    loads[6].wait()
    loads[7].wait()
    w32[...] = w_ref[...].astype(F32)
    w_c = jnp.concatenate(
        [w32[pl.ds(e, proj, stride=proj), :] for e in range(proj)], axis=1
    ).astype(BF16)
    w_e = jnp.concatenate(
        [w_ref[c * proj : (c + 1) * proj, :] for c in range(proj)], axis=1
    )

    def spread_left(gl, part):
        p = mm(gl[:, :proj], w_c).astype(BF16)
        for e in range(proj):
            for i in range(loc):
                p2[part * proj * seq + e * seq : part * proj * seq + (e + 1) * seq,
                   i * chan : (i + 1) * chan] = p[
                    i * seq : (i + 1) * seq, e * chan : (e + 1) * chan
                ]

    spread_left(g, 0)
    partner(0).wait_recv()
    gp = gp_r[...]
    spread_left(gp, 1)

    def arrivals(k):
        r = lax.rem(row + nrow - k, nrow)

        def same():
            copy(f_s.at[1], r_r.at[r], 1, r, r, dev(r, col)).wait_recv()
            copy(f_s.at[0], l_r.at[r], 0, r, r, dev(r, col)).wait_recv()
            copy(m_s, m_r.at[0, r], 4, r, r, dev(r, col)).wait_recv()
            on(
                half_of(row) == col,
                lambda: copy(ct_s.at[0], ct_r.at[r], 3, r, r, dev(r, col)).wait_recv(),
            )

        if isinstance(k, int):
            if k:
                same()
        else:
            on(k != 0, same)
        on(
            half_of(r) == col,
            lambda: copy(f_s.at[1], ro_r.at[r], 2, r, r, dev(r, other)).wait_recv(),
        )
        copy(m_s, m_r.at[1, r], 5, r, r, dev(r, other)).wait_recv()
        on(
            half_of(row) == other,
            lambda: copy(ct_s.at[0], ct_r.at[r], 6, r, r, dev(r, other)).wait_recv(),
        )

    partner(1).wait_recv()
    each(nrow, arrivals)

    rep = (iota((res, nrow), 0) >> lo == iota((res, nrow), 1)).astype(BF16)
    own_lane = (iota((res, 128), 0) & (loc - 1)) == (iota((res, 128), 1) >> sq)
    z = [
        jnp.where(own_lane, mm(rep, m_r[k].reshape(nrow, 128).astype(BF16)), 0.0).astype(BF16)
        for k in range(2)
    ]
    counts = []
    for b in range(loc):
        total = None
        for k, gl in enumerate((g, gp)):
            m_b = jnp.broadcast_to(
                gl[b * seq : (b + 1) * seq, 2 * proj : 2 * proj + 1].astype(F32), (seq, 128)
            ).astype(BF16)
            term = mm(z[k], jnp.concatenate([m_b] * (128 // seq), axis=0))
            total = term if total is None else total + term
        counts.append(jnp.maximum(total, 1.0))

    def unflatten(ref, n, start=0):
        return jnp.concatenate(
            [ref[pl.ds(start + t, n, stride=tiles), :] for t in range(tiles)], axis=1
        ).astype(BF16)

    a32[...] = r_r[...].astype(F32).reshape(res * tiles, 128)
    b32[...] = l_r[...].astype(F32).reshape(res * tiles, 128)
    c32[...] = ct_r[...].astype(F32).reshape(res * loc, 128)
    o32[...] = (
        ro_r[pl.ds(col * per_half, per_half)].astype(F32).reshape(half_res * tiles, 128)
    )
    right_all = unflatten(a32, res)
    left_all = unflatten(b32, res)

    start = pl.multiple_of(col * half_res * tiles, half_res * tiles)
    r_half = jnp.concatenate(
        [unflatten(a32, half_res, start), unflatten(o32, half_res)], axis=1
    )
    mapped = mm(r_half, p2[...])
    bias = bias_ref[...]
    for i in range(loc):
        w32[:res] = counts[i]
        div = w32[pl.ds(pl.multiple_of(col * half_res, half_res), half_res), :]
        pu_ref[i] = (mapped[:, i * chan : (i + 1) * chan] / div + bias).astype(BF16)

    def grad(flat, scaled, weight):
        q = lax.dot_general(
            flat, scaled, (((0,), (0,)), ((), ())), preferred_element_type=F32
        ).astype(BF16)
        for e in range(proj):
            for i in range(loc):
                q2[i * seq : (i + 1) * seq, e * chan : (e + 1) * chan] = q[
                    e * seq : (e + 1) * seq, i * chan : (i + 1) * chan
                ]
        return lax.dot_general(
            q2[...], weight, (((1,), (1,)), ((), ())), preferred_element_type=F32
        )

    scaled = jnp.concatenate(
        [(cf_r[i].astype(F32) / counts[i]).astype(BF16) for i in range(loc)], axis=1
    )
    lg_ref[...] = grad(right_all, scaled, w_c)
    scaled_t = jnp.concatenate(
        [
            (c32[pl.ds(j, res, stride=loc), :] / counts[j]).astype(BF16)
            for j in range(loc)
        ],
        axis=1,
    )
    rg_ref[...] = grad(left_all, scaled_t, w_e)

    partner(0).wait_send()
    partner(1).wait_send()
    each(nrow, lambda j: sends(nrow - 1 - j, lambda d: d.wait_send()))


def finish(pu_in, lg_in, rg_in, pu_ref, lg_ref, rg_ref):
    seq, loc, _ = lg_ref.shape
    pu_ref[...] = pu_in[...]
    for i in range(loc):
        lg_ref[:, i, :] = lg_in[i * seq : (i + 1) * seq, :]
        rg_ref[:, i, :] = rg_in[i * seq : (i + 1) * seq, :]


def per_device(nrow, x, am, rm, wl, wr, w, bias, cot):
    seq, loc, _ = x.shape
    proj = wl.shape[1]
    half_res, chan = cot.shape[1], cot.shape[2]
    res = nrow * loc
    tiles = proj * seq // 128
    fr = loc * tiles
    rows = loc * seq
    hbm = pl.BlockSpec(memory_space=pltpu.HBM)
    vm = pl.BlockSpec(memory_space=pltpu.VMEM)
    operands = (x, am.T, rm.reshape(1, loc), wl.T, wr.T, w, bias.reshape(1, chan), cot)
    held = [pltpu.with_memory_space_constraint(a, pltpu.HBM) for a in operands]
    pu, lg, rg = pl.pallas_call(
        functools.partial(kernel, nrow),
        out_shape=(
            jax.ShapeDtypeStruct(cot.shape, BF16),
            jax.ShapeDtypeStruct((rows, proj), F32),
            jax.ShapeDtypeStruct((rows, proj), F32),
        ),
        in_specs=[hbm] * 8,
        out_specs=(vm, vm, vm),
        scratch_shapes=[pltpu.VMEM(a.shape, a.dtype) for a in operands]
        + [
            pltpu.VMEM((rows, 128), BF16),
            pltpu.VMEM((rows, 128), BF16),
            pltpu.VMEM((2, fr, 128), BF16),
            pltpu.VMEM((nrow, fr, 128), BF16),
            pltpu.VMEM((nrow, fr, 128), BF16),
            pltpu.VMEM((nrow, fr, 128), BF16),
            pltpu.VMEM((half_res // loc, loc * loc, 128), BF16),
            pltpu.VMEM((nrow, loc * loc, 128), BF16),
            pltpu.VMEM((loc, res, chan), BF16),
            pltpu.VMEM((1, 128), F32),
            pltpu.VMEM((2, nrow, 1, 128), F32),
            pltpu.VMEM((max(proj * proj, res), chan), F32),
            pltpu.VMEM((res * tiles, 128), F32),
            pltpu.VMEM((res * tiles, 128), F32),
            pltpu.VMEM((half_res * tiles, 128), F32),
            pltpu.VMEM((res * loc, 128), F32),
            pltpu.VMEM((2 * proj * seq, loc * chan), BF16),
            pltpu.VMEM((rows, proj * chan), BF16),
            pltpu.SemaphoreType.DMA((7, nrow)),
            pltpu.SemaphoreType.DMA((7, nrow)),
            pltpu.SemaphoreType.DMA((4,)),
            pltpu.SemaphoreType.DMA((8,)),
        ],
        compiler_params=pltpu.CompilerParams(
            collective_id=0, has_side_effects=True, vmem_limit_bytes=GRANT
        ),
    )(*held)
    grads = jax.ShapeDtypeStruct((seq, loc, proj), F32)
    return pl.pallas_call(
        finish,
        out_shape=(jax.ShapeDtypeStruct(cot.shape, BF16), grads, grads),
        in_specs=[vm] * 3,
        out_specs=(vm, vm, vm),
        compiler_params=pltpu.CompilerParams(vmem_limit_bytes=GRANT),
    )(pu, lg, rg)


def solution(mesh):
    placed = (
        P(("grp", "col"), "row", None),
        P(("grp", "col"), "row"),
        P(("grp", "row")),
        P(),
        P(),
        P(),
        P(),
        P(("grp", "row"), "col", None),
    )
    return jax.shard_map(
        functools.partial(per_device, mesh.shape["row"]),
        mesh=mesh,
        in_specs=placed,
        out_specs=(
            P(("grp", "row"), "col", None),
            P(("grp", "col"), "row", None),
            P(("grp", "col"), "row", None),
        ),
        check_vma=False,
    )
```

```python
import functools

import jax
import jax.numpy as jnp
from jax import lax
from jax.experimental import pallas as pl
from jax.experimental.pallas import tpu as pltpu
from jax.sharding import PartitionSpec as P

F32 = jnp.float32
BF16 = jnp.bfloat16
MESH = pl.DeviceIdType.MESH
UNROLL = 8
GRANT = 24 << 20


def iota(shape, axis):
    return lax.broadcasted_iota(jnp.int32, shape, axis)


def mm(a, b):
    return lax.dot_general(a, b, (((1,), (0,)), ((), ())), preferred_element_type=F32)


def each(n, f):
    if n <= UNROLL:
        for k in range(n):
            f(k)
    else:

        @pl.loop(0, n)
        def _(k):
            f(k)


def kernel(
    nrow,
    x_hbm, am_hbm, rm_hbm, wl_hbm, wr_hbm, w_hbm, bias_hbm, cot_hbm,
    pu_ref, lg_ref, rg_ref,
    x_ref, am_ref, rm_ref, wl_ref, wr_ref, w_ref, bias_ref, cot_ref,
    g_s, gp_r, f_s, l_r, r_r, ro_r, ct_s, ct_r, cf_r, m_s, m_r,
    w32, a32, b32, o32, c32, p2, q2,
    ssem, rsem, psem, isem,
):
    seq, loc, feat = x_ref.shape
    proj = wl_ref.shape[0]
    half_res, chan = cot_ref.shape[1], cot_ref.shape[2]
    res = nrow * loc
    per_half = half_res // loc
    tiles = proj * seq // 128
    rows = loc * seq
    lo = loc.bit_length() - 1
    sq = seq.bit_length() - 1
    tl = tiles.bit_length() - 1

    grp, row, col = lax.axis_index("grp"), lax.axis_index("row"), lax.axis_index("col")
    other = 1 - col

    def half_of(r):
        return jnp.where(r >= per_half, 1, 0)

    def dev(r, c):
        return (grp, r, c)

    barrier = pltpu.get_barrier_semaphore()

    def peer(k):
        if nrow & (nrow - 1):
            return lax.rem(row + k, nrow)
        r = 0
        for b in range(nrow.bit_length() - 1):
            bit = lax.rem(lax.div(row, 1 << b) + k // (1 << b), 2)
            r = r + bit * (1 << b)
        return r

    def greet(j):
        k = nrow - 1 - j
        r = peer(k)
        pl.semaphore_signal(barrier, inc=1, device_id=dev(r, other), device_id_type=MESH)
        if isinstance(k, int):
            if k:
                pl.semaphore_signal(barrier, inc=1, device_id=dev(r, col), device_id_type=MESH)
        else:

            @pl.when(k != 0)
            def _():
                pl.semaphore_signal(barrier, inc=1, device_id=dev(r, col), device_id_type=MESH)

    each(nrow, greet)
    loads = [
        pltpu.make_async_copy(src, dst, isem.at[k])
        for k, (src, dst) in enumerate(
            (
                (x_hbm, x_ref), (wl_hbm, wl_ref), (wr_hbm, wr_ref), (am_hbm, am_ref),
                (rm_hbm, rm_ref), (cot_hbm, cot_ref), (w_hbm, w_ref), (bias_hbm, bias_ref),
            )
        )
    ]
    for load in loads:
        load.start()
    for load in loads[:6]:
        load.wait()

    xf = x_ref[...].astype(F32)
    x = jnp.concatenate([xf[:, r, :] for r in range(loc)], axis=0).astype(BF16)
    live = jnp.concatenate(
        [
            jnp.broadcast_to(
                (am_ref[r : r + 1, :] * rm_ref[:, r : r + 1]).astype(F32), (seq, seq)
            )
            for r in range(loc)
        ],
        axis=0,
    )
    diagonal = (iota((rows, seq), 0) & (seq - 1)) == iota((rows, seq), 1)
    live = jnp.sum(jnp.where(diagonal, live, 0.0), axis=1, keepdims=True)
    live = jnp.broadcast_to(live, (rows, 128))
    factors = jnp.concatenate(
        [wl_ref[...], wr_ref[...], jnp.zeros((128 - 2 * proj, feat), BF16)], axis=0
    )
    both = lax.dot_general(x, factors, (((1,), (1,)), ((), ())), preferred_element_type=F32)
    both = jnp.where(iota((rows, 128), 1) < 2 * proj, both, 1.0) * live
    g = both.astype(BF16)
    g_s[...] = g
    lane = iota((rows, 128), 1)
    at = iota((rows, 128), 0)
    m_s[...] = jnp.sum(jnp.where(lane == at, live, 0.0), axis=0, keepdims=True)
    width = 2 * proj * seq
    spread = (iota((128, width), 0) == (iota((128, width), 1) >> sq)).astype(BF16)
    own_seq = (iota((rows, width), 0) & (seq - 1)) == (iota((rows, width), 1) & (seq - 1))
    h = jnp.where(own_seq, mm(g, spread), 0.0).astype(BF16)
    h = jnp.concatenate([h[:, k * 128 : (k + 1) * 128] for k in range(2 * tiles)], axis=0)
    frows, deep = 2 * loc * tiles, 2 * tiles * rows
    fi, ki = iota((frows, deep), 0), iota((frows, deep), 1)
    f_x, f_r, f_t = fi >> (lo + tl), (fi >> tl) & (loc - 1), fi & (tiles - 1)
    k_x, k_t, k_r = ki >> (tl + lo + sq), (ki >> (lo + sq)) & (tiles - 1), (ki >> sq) & (loc - 1)
    pick = ((f_x == k_x) & (f_r == k_r) & (f_t == k_t)).astype(BF16)
    f = mm(pick, h).astype(BF16)
    fr = loc * tiles
    f_s[0] = f[:fr]
    f_s[1] = f[fr:]
    cot32 = cot_ref[...].astype(F32)
    for q in range(per_half if per_half <= UNROLL else 0):
        ct_s[q] = jnp.concatenate(
            [cot32[i, q * loc : (q + 1) * loc, :] for i in range(loc)], axis=0
        ).astype(BF16)
    if per_half > UNROLL:
        c32_rows = c32.shape[0] // loc

        for i in range(loc):
            c32[i * c32_rows : i * c32_rows + half_res] = cot32[i]

        @pl.loop(0, per_half)
        def _(q):
            ct_s[q] = jnp.concatenate(
                [
                    c32[pl.ds(i * c32_rows + q * loc, loc), :]
                    for i in range(loc)
                ],
                axis=0,
            ).astype(BF16)

    pl.semaphore_wait(barrier, 2 * nrow - 1)

    def copy(src, dst, kind, s_slot, r_slot, to):
        return pltpu.make_async_remote_copy(
            src_ref=src, dst_ref=dst, send_sem=ssem.at[kind, s_slot],
            recv_sem=rsem.at[kind, r_slot], device_id=to, device_id_type=MESH,
        )

    def partner(k):
        if k == 0:
            src, dst = g_s, gp_r
        else:
            src, dst = cot_ref, cf_r.at[:, pl.ds(pl.multiple_of(col * half_res, half_res), half_res), :]
        return pltpu.make_async_remote_copy(
            src_ref=src, dst_ref=dst, send_sem=psem.at[k], recv_sem=psem.at[2 + k],
            device_id=dev(row, other), device_id_type=MESH,
        )

    def on(pred, f):
        pl.when(pred)(f)

    def sends(k, phase, act):
        r = peer(k)
        q = jnp.where(r >= per_half, r - per_half, r)
        far = half_of(r) == col

        def same():
            if phase == 0:
                act(copy(m_s, m_r.at[0, row], 4, r, row, dev(r, col)))
                on(far, lambda: act(copy(ct_s.at[q], ct_r.at[row], 3, r, row, dev(r, col))))
            elif phase == 1:
                act(copy(f_s.at[1], r_r.at[row], 1, r, row, dev(r, col)))
            else:
                act(copy(f_s.at[0], l_r.at[row], 0, r, row, dev(r, col)))

        if isinstance(k, int):
            if k:
                same()
        else:
            on(k != 0, same)
        if phase == 0:
            act(copy(m_s, m_r.at[1, row], 5, r, row, dev(r, other)))
            on(far, lambda: act(copy(ct_s.at[q], ct_r.at[row], 6, r, row, dev(r, other))))
        elif phase == 1:
            on(
                half_of(row) == other,
                lambda: act(copy(f_s.at[1], ro_r.at[row], 2, r, row, dev(r, other))),
            )

    partner(0).start()
    partner(1).start()
    for phase in range(3):
        each(nrow, lambda j: sends(nrow - 1 - j, phase, lambda d: d.start()))

    l_r[row] = f[:fr]
    r_r[row] = f[fr:]
    m_r[0, row] = m_s[...]
    cf_r[:, pl.ds(pl.multiple_of(col * half_res, half_res), half_res), :] = cot_ref[...]

    @pl.when(half_of(row) == col)
    def _():
        ct_r[row] = ct_s[jnp.where(row >= per_half, row - per_half, row)]

    loads[6].wait()
    loads[7].wait()
    w32[: proj * proj] = w_ref[...].astype(F32)
    w_c = jnp.concatenate(
        [w32[pl.ds(e, proj, stride=proj), :] for e in range(proj)], axis=1
    ).astype(BF16)
    w_e = jnp.concatenate(
        [w_ref[c * proj : (c + 1) * proj, :] for c in range(proj)], axis=1
    )

    def spread_left(gl, part):
        p = mm(gl[:, :proj], w_c).astype(BF16)
        for e in range(proj):
            for i in range(loc):
                p2[part * proj * seq + e * seq : part * proj * seq + (e + 1) * seq,
                   i * chan : (i + 1) * chan] = p[
                    i * seq : (i + 1) * seq, e * chan : (e + 1) * chan
                ]

    spread_left(g, 0)
    partner(0).wait_recv()
    gp = gp_r[...]
    spread_left(gp, 1)

    def arrivals(k, phase):
        r = peer(k)

        def same():
            if phase == 0:
                copy(m_s, m_r.at[0, r], 4, r, r, dev(r, col)).wait_recv()
                on(
                    half_of(row) == col,
                    lambda: copy(ct_s.at[0], ct_r.at[r], 3, r, r, dev(r, col)).wait_recv(),
                )
            elif phase == 1:
                copy(f_s.at[1], r_r.at[r], 1, r, r, dev(r, col)).wait_recv()
            else:
                copy(f_s.at[0], l_r.at[r], 0, r, r, dev(r, col)).wait_recv()

        if isinstance(k, int):
            if k:
                same()
        else:
            on(k != 0, same)
        if phase == 0:
            copy(m_s, m_r.at[1, r], 5, r, r, dev(r, other)).wait_recv()
            on(
                half_of(row) == other,
                lambda: copy(ct_s.at[0], ct_r.at[r], 6, r, r, dev(r, other)).wait_recv(),
            )
        elif phase == 1:
            on(
                half_of(r) == col,
                lambda: copy(f_s.at[1], ro_r.at[r], 2, r, r, dev(r, other)).wait_recv(),
            )

    partner(1).wait_recv()
    each(nrow, lambda k: arrivals(k, 0))

    rep = (iota((res, nrow), 0) >> lo == iota((res, nrow), 1)).astype(BF16)
    own_lane = (iota((res, 128), 0) & (loc - 1)) == (iota((res, 128), 1) >> sq)
    z = [
        jnp.where(own_lane, mm(rep, m_r[k].reshape(nrow, 128).astype(BF16)), 0.0).astype(BF16)
        for k in range(2)
    ]
    counts = []
    for b in range(loc):
        total = None
        for k, gl in enumerate((g, gp)):
            m_b = jnp.broadcast_to(
                gl[b * seq : (b + 1) * seq, 2 * proj : 2 * proj + 1].astype(F32), (seq, 128)
            ).astype(BF16)
            term = mm(z[k], jnp.concatenate([m_b] * (128 // seq), axis=0))
            total = term if total is None else total + term
        counts.append(jnp.maximum(total, 1.0))

    def unflatten(ref, n, start=0):
        return jnp.concatenate(
            [ref[pl.ds(start + t, n, stride=tiles), :] for t in range(tiles)], axis=1
        ).astype(BF16)

    c32[...] = ct_r[...].astype(F32).reshape(res * loc, 128)
    scaled = jnp.concatenate(
        [(cf_r[i].astype(F32) / counts[i]).astype(BF16) for i in range(loc)], axis=1
    )
    scaled_t = jnp.concatenate(
        [
            (c32[pl.ds(j, res, stride=loc), :] / counts[j]).astype(BF16)
            for j in range(loc)
        ],
        axis=1,
    )
    for i in range(loc):
        w32[i * res : (i + 1) * res] = 1.0 / counts[i]

    each(nrow, lambda k: arrivals(k, 1))
    a32[...] = r_r[...].astype(F32).reshape(res * tiles, 128)
    o32[...] = (
        ro_r[pl.ds(col * per_half, per_half)].astype(F32).reshape(half_res * tiles, 128)
    )
    right_all = unflatten(a32, res)
    start = pl.multiple_of(col * half_res * tiles, half_res * tiles)
    r_half = jnp.concatenate(
        [unflatten(a32, half_res, start), unflatten(o32, half_res)], axis=1
    )
    mapped = mm(r_half, p2[...])
    bias = bias_ref[...]
    for i in range(loc):
        inverse = w32[pl.ds(pl.multiple_of(i * res + col * half_res, half_res), half_res), :]
        pu_ref[i] = (mapped[:, i * chan : (i + 1) * chan] * inverse + bias).astype(BF16)

    def grad(flat, scaled, weight):
        q = lax.dot_general(
            flat, scaled, (((0,), (0,)), ((), ())), preferred_element_type=F32
        ).astype(BF16)
        for e in range(proj):
            for i in range(loc):
                q2[i * seq : (i + 1) * seq, e * chan : (e + 1) * chan] = q[
                    e * seq : (e + 1) * seq, i * chan : (i + 1) * chan
                ]
        return lax.dot_general(
            q2[...], weight, (((1,), (1,)), ((), ())), preferred_element_type=F32
        )

    lg_ref[...] = grad(right_all, scaled, w_c)
    each(nrow, lambda k: arrivals(k, 2))
    b32[...] = l_r[...].astype(F32).reshape(res * tiles, 128)
    rg_ref[...] = grad(unflatten(b32, res), scaled_t, w_e)

    partner(0).wait_send()
    partner(1).wait_send()
    for phase in range(3):
        each(nrow, lambda j: sends(nrow - 1 - j, phase, lambda d: d.wait_send()))


def finish(pu_in, lg_in, rg_in, pu_ref, lg_ref, rg_ref):
    seq, loc, _ = lg_ref.shape
    pu_ref[...] = pu_in[...]
    for i in range(loc):
        lg_ref[:, i, :] = lg_in[i * seq : (i + 1) * seq, :]
        rg_ref[:, i, :] = rg_in[i * seq : (i + 1) * seq, :]


def per_device(nrow, x, am, rm, wl, wr, w, bias, cot):
    seq, loc, _ = x.shape
    proj = wl.shape[1]
    half_res, chan = cot.shape[1], cot.shape[2]
    res = nrow * loc
    tiles = proj * seq // 128
    fr = loc * tiles
    rows = loc * seq
    hbm = pl.BlockSpec(memory_space=pltpu.HBM)
    vm = pl.BlockSpec(memory_space=pltpu.VMEM)
    operands = (x, am.T, rm.reshape(1, loc), wl.T, wr.T, w, bias.reshape(1, chan), cot)
    held = [pltpu.with_memory_space_constraint(a, pltpu.HBM) for a in operands]
    pu, lg, rg = pl.pallas_call(
        functools.partial(kernel, nrow),
        out_shape=(
            jax.ShapeDtypeStruct(cot.shape, BF16),
            jax.ShapeDtypeStruct((rows, proj), F32),
            jax.ShapeDtypeStruct((rows, proj), F32),
        ),
        in_specs=[hbm] * 8,
        out_specs=(vm, vm, vm),
        scratch_shapes=[pltpu.VMEM(a.shape, a.dtype) for a in operands]
        + [
            pltpu.VMEM((rows, 128), BF16),
            pltpu.VMEM((rows, 128), BF16),
            pltpu.VMEM((2, fr, 128), BF16),
            pltpu.VMEM((nrow, fr, 128), BF16),
            pltpu.VMEM((nrow, fr, 128), BF16),
            pltpu.VMEM((nrow, fr, 128), BF16),
            pltpu.VMEM((half_res // loc, loc * loc, 128), BF16),
            pltpu.VMEM((nrow, loc * loc, 128), BF16),
            pltpu.VMEM((loc, res, chan), BF16),
            pltpu.VMEM((1, 128), F32),
            pltpu.VMEM((2, nrow, 1, 128), F32),
            pltpu.VMEM((max(proj * proj, loc * res), chan), F32),
            pltpu.VMEM((res * tiles, 128), F32),
            pltpu.VMEM((res * tiles, 128), F32),
            pltpu.VMEM((half_res * tiles, 128), F32),
            pltpu.VMEM((res * loc, 128), F32),
            pltpu.VMEM((2 * proj * seq, loc * chan), BF16),
            pltpu.VMEM((rows, proj * chan), BF16),
            pltpu.SemaphoreType.DMA((7, nrow)),
            pltpu.SemaphoreType.DMA((7, nrow)),
            pltpu.SemaphoreType.DMA((4,)),
            pltpu.SemaphoreType.DMA((8,)),
        ],
        compiler_params=pltpu.CompilerParams(
            collective_id=0, has_side_effects=True, vmem_limit_bytes=GRANT
        ),
    )(*held)
    grads = jax.ShapeDtypeStruct((seq, loc, proj), F32)
    return pl.pallas_call(
        finish,
        out_shape=(jax.ShapeDtypeStruct(cot.shape, BF16), grads, grads),
        in_specs=[vm] * 3,
        out_specs=(vm, vm, vm),
        compiler_params=pltpu.CompilerParams(vmem_limit_bytes=GRANT),
    )(pu, lg, rg)


def solution(mesh):
    placed = (
        P(("grp", "col"), "row", None),
        P(("grp", "col"), "row"),
        P(("grp", "row")),
        P(),
        P(),
        P(),
        P(),
        P(("grp", "row"), "col", None),
    )
    return jax.shard_map(
        functools.partial(per_device, mesh.shape["row"]),
        mesh=mesh,
        in_specs=placed,
        out_specs=(
            P(("grp", "row"), "col", None),
            P(("grp", "col"), "row", None),
            P(("grp", "col"), "row", None),
        ),
        check_vma=False,
    )
```

```python
import functools

import jax
import jax.numpy as jnp
from jax import lax
from jax.experimental import pallas as pl
from jax.experimental.pallas import tpu as pltpu
from jax.sharding import PartitionSpec as P

F32 = jnp.float32
BF16 = jnp.bfloat16
MESH = pl.DeviceIdType.MESH
UNROLL = 8
GRANT = 24 << 20


def iota(shape, axis):
    return lax.broadcasted_iota(jnp.int32, shape, axis)


def mm(a, b):
    return lax.dot_general(a, b, (((1,), (0,)), ((), ())), preferred_element_type=F32)


def each(n, f):
    if n <= UNROLL:
        for k in range(n):
            f(k)
    else:

        @pl.loop(0, n)
        def _(k):
            f(k)


def kernel(
    nrow,
    x_hbm, am_hbm, rm_hbm, wl_hbm, wr_hbm, w_hbm, bias_hbm, cot_hbm,
    pu_ref, lg_ref, rg_ref,
    x_ref, am_ref, rm_ref, wl_ref, wr_ref, w_ref, bias_ref, cot_ref,
    g_s, gp_r, f_s, l_r, r_r, ro_r, ct_s, ct_r, cf_r, m_s, m_r,
    w32, a32, b32, o32, c32, p2, q2,
    ssem, rsem, psem, isem,
):
    seq, loc, feat = x_ref.shape
    proj = wl_ref.shape[0]
    half_res, chan = cot_ref.shape[1], cot_ref.shape[2]
    res = nrow * loc
    per_half = half_res // loc
    tiles = proj * seq // 128
    rows = loc * seq
    lo = loc.bit_length() - 1
    sq = seq.bit_length() - 1
    tl = tiles.bit_length() - 1

    grp, row, col = lax.axis_index("grp"), lax.axis_index("row"), lax.axis_index("col")
    other = 1 - col

    def half_of(r):
        return jnp.where(r >= per_half, 1, 0)

    def dev(r, c):
        return (grp, r, c)

    barrier = pltpu.get_barrier_semaphore()

    def peer(k):
        if nrow & (nrow - 1):
            return lax.rem(row + k, nrow)
        r = 0
        for b in range(nrow.bit_length() - 1):
            bit = lax.rem(lax.div(row, 1 << b) + k // (1 << b), 2)
            r = r + bit * (1 << b)
        return r

    def greet(j):
        k = nrow - 1 - j
        r = peer(k)
        pl.semaphore_signal(barrier, inc=1, device_id=dev(r, other), device_id_type=MESH)
        if isinstance(k, int):
            if k:
                pl.semaphore_signal(barrier, inc=1, device_id=dev(r, col), device_id_type=MESH)
        else:

            @pl.when(k != 0)
            def _():
                pl.semaphore_signal(barrier, inc=1, device_id=dev(r, col), device_id_type=MESH)

    each(nrow, greet)
    loads = [
        pltpu.make_async_copy(src, dst, isem.at[k])
        for k, (src, dst) in enumerate(
            (
                (x_hbm, x_ref), (wl_hbm, wl_ref), (wr_hbm, wr_ref), (am_hbm, am_ref),
                (rm_hbm, rm_ref), (cot_hbm, cot_ref), (w_hbm, w_ref), (bias_hbm, bias_ref),
            )
        )
    ]
    for load in loads:
        load.start()
    for load in loads[:6]:
        load.wait()

    xf = x_ref[...].astype(F32)
    x = jnp.concatenate([xf[:, r, :] for r in range(loc)], axis=0).astype(BF16)
    live = jnp.concatenate(
        [
            jnp.broadcast_to(
                (am_ref[r : r + 1, :] * rm_ref[:, r : r + 1]).astype(F32), (seq, seq)
            )
            for r in range(loc)
        ],
        axis=0,
    )
    diagonal = (iota((rows, seq), 0) & (seq - 1)) == iota((rows, seq), 1)
    live = jnp.sum(jnp.where(diagonal, live, 0.0), axis=1, keepdims=True)
    live = jnp.broadcast_to(live, (rows, 128))
    factors = jnp.concatenate(
        [wl_ref[...], wr_ref[...], jnp.zeros((128 - 2 * proj, feat), BF16)], axis=0
    )
    both = lax.dot_general(x, factors, (((1,), (1,)), ((), ())), preferred_element_type=F32)
    both = jnp.where(iota((rows, 128), 1) < 2 * proj, both, 1.0) * live
    g = both.astype(BF16)
    g_s[...] = g
    lane = iota((rows, 128), 1)
    at = iota((rows, 128), 0)
    m_s[...] = jnp.sum(jnp.where(lane == at, live, 0.0), axis=0, keepdims=True)
    width = 2 * proj * seq
    spread = (iota((128, width), 0) == (iota((128, width), 1) >> sq)).astype(BF16)
    own_seq = (iota((rows, width), 0) & (seq - 1)) == (iota((rows, width), 1) & (seq - 1))
    h = jnp.where(own_seq, mm(g, spread), 0.0).astype(BF16)
    h = jnp.concatenate([h[:, k * 128 : (k + 1) * 128] for k in range(2 * tiles)], axis=0)
    frows, deep = 2 * loc * tiles, 2 * tiles * rows
    fi, ki = iota((frows, deep), 0), iota((frows, deep), 1)
    f_x, f_r, f_t = fi >> (lo + tl), (fi >> tl) & (loc - 1), fi & (tiles - 1)
    k_x, k_t, k_r = ki >> (tl + lo + sq), (ki >> (lo + sq)) & (tiles - 1), (ki >> sq) & (loc - 1)
    pick = ((f_x == k_x) & (f_r == k_r) & (f_t == k_t)).astype(BF16)
    f = mm(pick, h).astype(BF16)
    fr = loc * tiles
    f_s[0] = f[:fr]
    f_s[1] = f[fr:]
    cot32 = cot_ref[...].astype(F32)
    for q in range(per_half if per_half <= UNROLL else 0):
        ct_s[q] = jnp.concatenate(
            [cot32[i, q * loc : (q + 1) * loc, :] for i in range(loc)], axis=0
        ).astype(BF16)
    if per_half > UNROLL:
        c32_rows = c32.shape[0] // loc

        for i in range(loc):
            c32[i * c32_rows : i * c32_rows + half_res] = cot32[i]

        @pl.loop(0, per_half)
        def _(q):
            ct_s[q] = jnp.concatenate(
                [
                    c32[pl.ds(i * c32_rows + q * loc, loc), :]
                    for i in range(loc)
                ],
                axis=0,
            ).astype(BF16)

    pl.semaphore_wait(barrier, 2 * nrow - 1)

    def copy(src, dst, kind, s_slot, r_slot, to):
        return pltpu.make_async_remote_copy(
            src_ref=src, dst_ref=dst, send_sem=ssem.at[kind, s_slot],
            recv_sem=rsem.at[kind, r_slot], device_id=to, device_id_type=MESH,
        )

    def partner(k):
        if k == 0:
            src, dst = g_s, gp_r
        else:
            src, dst = cot_ref, cf_r.at[:, pl.ds(pl.multiple_of(col * half_res, half_res), half_res), :]
        return pltpu.make_async_remote_copy(
            src_ref=src, dst_ref=dst, send_sem=psem.at[k], recv_sem=psem.at[2 + k],
            device_id=dev(row, other), device_id_type=MESH,
        )

    def on(pred, f):
        pl.when(pred)(f)

    def sends(k, phase, act):
        r = peer(k)
        q = jnp.where(r >= per_half, r - per_half, r)
        far = half_of(r) == col

        def same():
            if phase == 0:
                act(copy(m_s, m_r.at[0, row], 4, r, row, dev(r, col)))
                on(far, lambda: act(copy(ct_s.at[q], ct_r.at[row], 3, r, row, dev(r, col))))
            elif phase == 1:
                act(copy(f_s.at[0], l_r.at[row], 0, r, row, dev(r, col)))
            elif phase == 2:
                act(copy(f_s.at[1], r_r.at[row], 1, r, row, dev(r, col)))

        if isinstance(k, int):
            if k:
                same()
        else:
            on(k != 0, same)
        if phase == 0:
            act(copy(m_s, m_r.at[1, row], 5, r, row, dev(r, other)))
            on(far, lambda: act(copy(ct_s.at[q], ct_r.at[row], 6, r, row, dev(r, other))))
        elif phase == 3:
            on(
                half_of(row) == other,
                lambda: act(copy(f_s.at[1], ro_r.at[row], 2, r, row, dev(r, other))),
            )

    partner(0).start()
    partner(1).start()
    for phase in range(4):
        each(nrow, lambda j: sends(nrow - 1 - j, phase, lambda d: d.start()))

    l_r[row] = f[:fr]
    r_r[row] = f[fr:]
    m_r[0, row] = m_s[...]
    cf_r[:, pl.ds(pl.multiple_of(col * half_res, half_res), half_res), :] = cot_ref[...]

    @pl.when(half_of(row) == col)
    def _():
        ct_r[row] = ct_s[jnp.where(row >= per_half, row - per_half, row)]

    loads[6].wait()
    loads[7].wait()
    w32[: proj * proj] = w_ref[...].astype(F32)
    w_c = jnp.concatenate(
        [w32[pl.ds(e, proj, stride=proj), :] for e in range(proj)], axis=1
    ).astype(BF16)
    w_e = jnp.concatenate(
        [w_ref[c * proj : (c + 1) * proj, :] for c in range(proj)], axis=1
    )

    def spread_left(gl, part):
        p = mm(gl[:, :proj], w_c).astype(BF16)
        for e in range(proj):
            for i in range(loc):
                p2[part * proj * seq + e * seq : part * proj * seq + (e + 1) * seq,
                   i * chan : (i + 1) * chan] = p[
                    i * seq : (i + 1) * seq, e * chan : (e + 1) * chan
                ]

    spread_left(g, 0)
    partner(0).wait_recv()
    gp = gp_r[...]
    spread_left(gp, 1)

    def arrivals(k, phase):
        r = peer(k)

        def same():
            if phase == 0:
                copy(m_s, m_r.at[0, r], 4, r, r, dev(r, col)).wait_recv()
                on(
                    half_of(row) == col,
                    lambda: copy(ct_s.at[0], ct_r.at[r], 3, r, r, dev(r, col)).wait_recv(),
                )
            elif phase == 1:
                copy(f_s.at[0], l_r.at[r], 0, r, r, dev(r, col)).wait_recv()
            elif phase == 2:
                copy(f_s.at[1], r_r.at[r], 1, r, r, dev(r, col)).wait_recv()

        if isinstance(k, int):
            if k:
                same()
        else:
            on(k != 0, same)
        if phase == 0:
            copy(m_s, m_r.at[1, r], 5, r, r, dev(r, other)).wait_recv()
            on(
                half_of(row) == other,
                lambda: copy(ct_s.at[0], ct_r.at[r], 6, r, r, dev(r, other)).wait_recv(),
            )
        elif phase == 3:
            on(
                half_of(r) == col,
                lambda: copy(f_s.at[1], ro_r.at[r], 2, r, r, dev(r, other)).wait_recv(),
            )

    partner(1).wait_recv()
    each(nrow, lambda k: arrivals(k, 0))

    rep = (iota((res, nrow), 0) >> lo == iota((res, nrow), 1)).astype(BF16)
    own_lane = (iota((res, 128), 0) & (loc - 1)) == (iota((res, 128), 1) >> sq)
    z = [
        jnp.where(own_lane, mm(rep, m_r[k].reshape(nrow, 128).astype(BF16)), 0.0).astype(BF16)
        for k in range(2)
    ]
    counts = []
    for b in range(loc):
        total = None
        for k, gl in enumerate((g, gp)):
            m_b = jnp.broadcast_to(
                gl[b * seq : (b + 1) * seq, 2 * proj : 2 * proj + 1].astype(F32), (seq, 128)
            ).astype(BF16)
            term = mm(z[k], jnp.concatenate([m_b] * (128 // seq), axis=0))
            total = term if total is None else total + term
        counts.append(jnp.maximum(total, 1.0))

    def unflatten(ref, n, start=0):
        return jnp.concatenate(
            [ref[pl.ds(start + t, n, stride=tiles), :] for t in range(tiles)], axis=1
        ).astype(BF16)

    c32[...] = ct_r[...].astype(F32).reshape(res * loc, 128)
    scaled = jnp.concatenate(
        [(cf_r[i].astype(F32) / counts[i]).astype(BF16) for i in range(loc)], axis=1
    )
    scaled_t = jnp.concatenate(
        [
            (c32[pl.ds(j, res, stride=loc), :] / counts[j]).astype(BF16)
            for j in range(loc)
        ],
        axis=1,
    )
    for i in range(loc):
        w32[i * res : (i + 1) * res] = 1.0 / counts[i]

    def grad(flat, scaled, weight):
        q = lax.dot_general(
            flat, scaled, (((0,), (0,)), ((), ())), preferred_element_type=F32
        ).astype(BF16)
        for e in range(proj):
            for i in range(loc):
                q2[i * seq : (i + 1) * seq, e * chan : (e + 1) * chan] = q[
                    e * seq : (e + 1) * seq, i * chan : (i + 1) * chan
                ]
        return lax.dot_general(
            q2[...], weight, (((1,), (1,)), ((), ())), preferred_element_type=F32
        )

    each(nrow, lambda k: arrivals(k, 1))
    b32[...] = l_r[...].astype(F32).reshape(res * tiles, 128)
    rg_ref[...] = grad(unflatten(b32, res), scaled_t, w_e)

    each(nrow, lambda k: arrivals(k, 2))
    a32[...] = r_r[...].astype(F32).reshape(res * tiles, 128)
    lg_ref[...] = grad(unflatten(a32, res), scaled, w_c)

    start = pl.multiple_of(col * half_res * tiles, half_res * tiles)
    deep = proj * seq
    mapped = mm(unflatten(a32, half_res, start), p2[:deep])
    bias = bias_ref[...]
    each(nrow, lambda k: arrivals(k, 3))
    o32[...] = (
        ro_r[pl.ds(col * per_half, per_half)].astype(F32).reshape(half_res * tiles, 128)
    )
    mapped = mapped + mm(unflatten(o32, half_res), p2[deep:])
    for i in range(loc):
        inverse = w32[pl.ds(pl.multiple_of(i * res + col * half_res, half_res), half_res), :]
        pu_ref[i] = (mapped[:, i * chan : (i + 1) * chan] * inverse + bias).astype(BF16)

    partner(0).wait_send()
    partner(1).wait_send()
    for phase in range(4):
        each(nrow, lambda j: sends(nrow - 1 - j, phase, lambda d: d.wait_send()))


def finish(pu_in, lg_in, rg_in, pu_ref, lg_ref, rg_ref):
    seq, loc, _ = lg_ref.shape
    pu_ref[...] = pu_in[...]
    for i in range(loc):
        lg_ref[:, i, :] = lg_in[i * seq : (i + 1) * seq, :]
        rg_ref[:, i, :] = rg_in[i * seq : (i + 1) * seq, :]


def per_device(nrow, x, am, rm, wl, wr, w, bias, cot):
    seq, loc, _ = x.shape
    proj = wl.shape[1]
    half_res, chan = cot.shape[1], cot.shape[2]
    res = nrow * loc
    tiles = proj * seq // 128
    fr = loc * tiles
    rows = loc * seq
    hbm = pl.BlockSpec(memory_space=pltpu.HBM)
    vm = pl.BlockSpec(memory_space=pltpu.VMEM)
    operands = (x, am.T, rm.reshape(1, loc), wl.T, wr.T, w, bias.reshape(1, chan), cot)
    held = [pltpu.with_memory_space_constraint(a, pltpu.HBM) for a in operands]
    pu, lg, rg = pl.pallas_call(
        functools.partial(kernel, nrow),
        out_shape=(
            jax.ShapeDtypeStruct(cot.shape, BF16),
            jax.ShapeDtypeStruct((rows, proj), F32),
            jax.ShapeDtypeStruct((rows, proj), F32),
        ),
        in_specs=[hbm] * 8,
        out_specs=(vm, vm, vm),
        scratch_shapes=[pltpu.VMEM(a.shape, a.dtype) for a in operands]
        + [
            pltpu.VMEM((rows, 128), BF16),
            pltpu.VMEM((rows, 128), BF16),
            pltpu.VMEM((2, fr, 128), BF16),
            pltpu.VMEM((nrow, fr, 128), BF16),
            pltpu.VMEM((nrow, fr, 128), BF16),
            pltpu.VMEM((nrow, fr, 128), BF16),
            pltpu.VMEM((half_res // loc, loc * loc, 128), BF16),
            pltpu.VMEM((nrow, loc * loc, 128), BF16),
            pltpu.VMEM((loc, res, chan), BF16),
            pltpu.VMEM((1, 128), F32),
            pltpu.VMEM((2, nrow, 1, 128), F32),
            pltpu.VMEM((max(proj * proj, loc * res), chan), F32),
            pltpu.VMEM((res * tiles, 128), F32),
            pltpu.VMEM((res * tiles, 128), F32),
            pltpu.VMEM((half_res * tiles, 128), F32),
            pltpu.VMEM((res * loc, 128), F32),
            pltpu.VMEM((2 * proj * seq, loc * chan), BF16),
            pltpu.VMEM((rows, proj * chan), BF16),
            pltpu.SemaphoreType.DMA((7, nrow)),
            pltpu.SemaphoreType.DMA((7, nrow)),
            pltpu.SemaphoreType.DMA((4,)),
            pltpu.SemaphoreType.DMA((8,)),
        ],
        compiler_params=pltpu.CompilerParams(
            collective_id=0, has_side_effects=True, vmem_limit_bytes=GRANT
        ),
    )(*held)
    grads = jax.ShapeDtypeStruct((seq, loc, proj), F32)
    return pl.pallas_call(
        finish,
        out_shape=(jax.ShapeDtypeStruct(cot.shape, BF16), grads, grads),
        in_specs=[vm] * 3,
        out_specs=(vm, vm, vm),
        compiler_params=pltpu.CompilerParams(vmem_limit_bytes=GRANT),
    )(pu, lg, rg)


def solution(mesh):
    placed = (
        P(("grp", "col"), "row", None),
        P(("grp", "col"), "row"),
        P(("grp", "row")),
        P(),
        P(),
        P(),
        P(),
        P(("grp", "row"), "col", None),
    )
    return jax.shard_map(
        functools.partial(per_device, mesh.shape["row"]),
        mesh=mesh,
        in_specs=placed,
        out_specs=(
            P(("grp", "row"), "col", None),
            P(("grp", "col"), "row", None),
            P(("grp", "col"), "row", None),
        ),
        check_vma=False,
    )
```
